32 devices in a mesh: grp: 2 (over y), chan: 4 (over z), day: 2 (over x), seg: 2 (over core).
Axes of the slice: x: 2, y: 2, z: 4, core: 2. Of those that a mesh axis runs over, the one named last changes fastest.
Arguments:
- records: bfloat16 [4, 4, 512, 2048], P('day', 'seg', ('grp', 'chan')), parts along dimension 2, may hold values from -30 to 30
- visits: int32 [3, 2, 512], P(None, None, ('grp', 'chan')), parts along dimension 2, may hold values from 0 to 63
Outputs:
- correlation: bfloat16 [256, 3, 2, 512], P(('day', 'seg'), None, None, ('grp', 'chan')), parts along dimension 3
The draws below stay inside these ranges and needn't reach their ends.
There are 2 independent parts, one for each index of `grp`. The reference program is written for one: setup_inputs(seed, part) draws one part's arguments, and reference() takes and returns one part's arrays. A program takes and returns all parts, laid end to end along the dimension named above; each array names one. Nothing has to cross between parts.
All inputs are finite; a program needn't handle non-finite values.
Results may differ from the reference program's by a relative error of at most 0.0068.
Values may be sent and summed in bfloat16 or wider, within the bound.
No kernel may reach another device: no remote copies, remote signals or barrier semaphores. Data moves between devices by JAX's collectives and lax.ppermute only.
A program may use at most 64 MiB of HBM per device.

```python
import math
import jax
import jax.numpy as jnp
from jax import lax

NS = 2048
FREQS = 512
BAND = 64
LAGS = 256
SEGS = 4
PICKS = 2
CH_DEV = 64
DAY_DEV = 2
BLOCKS = 4
C = 256
DAYS = 4
SEG_DEV = 2
REACH = 1
VISITS = 3
N_DAY = 2
N_SEG = 2


def draw_records(key, part):
    subkeys = jax.random.split(key, 6)
    full_shape = (DAYS, SEGS, C, NS)
    row_shape = (DAYS, SEGS, C, 1)
    tone_bin = jax.random.randint(subkeys[0], row_shape, 0, FREQS)
    sample_index = lax.broadcasted_iota(jnp.int32, full_shape, 3)
    phase_shift = jax.random.uniform(subkeys[1], row_shape, jnp.float32, -math.pi, math.pi)
    amplitude = jax.random.uniform(subkeys[2], row_shape, jnp.float32, 1.0, 3.0)
    tone_wave = amplitude * jnp.sin((tone_bin * sample_index % NS).astype(jnp.float32) * (2.0 * math.pi / NS) + phase_shift)
    noise_part = jnp.clip(jax.random.normal(subkeys[3], full_shape, jnp.float32), -5.0, 5.0)
    row_scale = jnp.exp(jax.random.uniform(subkeys[5], row_shape, jnp.float32, math.log(0.3), math.log(3.0)))
    return (row_scale * (noise_part + tone_wave)).astype(jnp.bfloat16)


def touch_ends(entries, key, low, high):
    dims = entries.shape
    place = [jax.random.randint(jax.random.fold_in(key, axis), (), 0, dims[axis]) for axis in range(len(dims))]
    entries = entries.at[tuple(place)].set(low)
    longest = dims.index(max(dims))
    place[longest] = (place[longest] + 1) % dims[longest]
    return entries.at[tuple(place)].set(high)


def setup_inputs(seed: int = 0, part: int = 0) -> dict:
    splits = jax.random.split(jax.random.key(seed), 3)
    part_keys = jax.random.split(jax.random.fold_in(splits[2], part), 3)
    return {
        "records": draw_records(jax.random.fold_in(jax.random.fold_in(splits[2], part), 71), part),
        "visits": touch_ends(jax.random.randint(part_keys[1], (VISITS, PICKS, C), 0, CH_DEV), jax.random.fold_in(part_keys[1], 1), 0, CH_DEV - 1).astype(jnp.int32),
    }


def forward_table():
    sample_index = lax.broadcasted_iota(jnp.int32, (NS, FREQS), 0)
    freq_index = lax.broadcasted_iota(jnp.int32, (NS, FREQS), 1)
    turns = (sample_index * freq_index % NS).astype(jnp.float32) * (2.0 * math.pi / NS)
    return jnp.concatenate([jnp.cos(turns), -jnp.sin(turns)], 1).astype(jnp.bfloat16)

def inverse_table():
    lag_index = lax.broadcasted_iota(jnp.int32, (LAGS, FREQS), 0) - LAGS // 2
    freq_index = lax.broadcasted_iota(jnp.int32, (LAGS, FREQS), 1)
    turns = (lag_index * freq_index % NS).astype(jnp.float32) * (2.0 * math.pi / NS)
    return jnp.concatenate([jnp.cos(turns), -jnp.sin(turns)], 1).astype(jnp.bfloat16)

def whiten(spectra):
    row_total = spectra.shape[0]
    real_part = spectra[:, :FREQS]
    imag_part = spectra[:, FREQS:]
    band_power = lax.optimization_barrier(jnp.mean((real_part * real_part + imag_part * imag_part).reshape(row_total, FREQS // BAND, BAND), axis=-1)) * 0.5
    factor = jnp.repeat(1.0 / jnp.sqrt(band_power + 1e-06), BAND, axis=1)
    return jnp.concatenate([real_part * factor, imag_part * factor], 1).astype(jnp.bfloat16)

def pair_spectrum(own_block, held_block, picked):
    source_rows = jnp.take(held_block, picked, axis=1)
    own_real = own_block[:, None, :, :FREQS].astype(jnp.float32)
    own_imag = own_block[:, None, :, FREQS:].astype(jnp.float32)
    other_real = source_rows[..., :FREQS].astype(jnp.float32)
    other_imag = source_rows[..., FREQS:].astype(jnp.float32)
    real_sum = lax.optimization_barrier(jnp.sum(own_real * other_real + own_imag * other_imag, axis=0))
    imag_sum = lax.optimization_barrier(jnp.sum(own_real * other_imag - own_imag * other_real, axis=0))
    return jnp.concatenate([real_sum, imag_sum], -1).astype(jnp.bfloat16)

def lag_terms(flat_rows, table_rows):
    return lax.dot_general(table_rows, flat_rows, (((1,), (1,)), ((), ())), preferred_element_type=jnp.float32)

def reference(records, visits):
    table = forward_table()

    def one_day(day_rows):
        spectra = jnp.dot(day_rows.reshape(SEGS * C, NS), table, preferred_element_type=jnp.float32)
        return whiten(spectra).reshape(SEGS, C, 2 * FREQS)
    whitened = lax.map(one_day, records)
    receiver_block = (jnp.arange(C) // CH_DEV).astype(jnp.int32)
    visit_index = jnp.arange(VISITS).astype(jnp.int32)[:, None, None]
    source = ((receiver_block[None, None, :] + REACH - visit_index) % BLOCKS * CH_DEV + visits).astype(jnp.int32)
    inverse = inverse_table()

    def group_term(group, total):
        day_first = (group // N_SEG * DAY_DEV).astype(jnp.int32)
        seg_first = (group % N_SEG * SEG_DEV).astype(jnp.int32)
        zero_index = jnp.zeros((), jnp.int32)
        block = lax.dynamic_slice(whitened, (day_first, seg_first, zero_index, zero_index), (DAY_DEV, SEG_DEV, C, 2 * FREQS))
        block = block.reshape(DAY_DEV * SEG_DEV, C, 2 * FREQS)
        cross_all = lax.map(lambda picked: pair_spectrum(block, block, picked), source)
        return total + lag_terms(cross_all.reshape(-1, 2 * FREQS), inverse)
    total = lax.fori_loop(0, N_DAY * N_SEG, group_term, jnp.zeros((LAGS, VISITS * PICKS * C), jnp.float32))
    scale_factor = 1.0 / math.sqrt(FREQS * DAYS * SEGS)
    return (total * scale_factor).astype(jnp.bfloat16).reshape(LAGS, VISITS, PICKS, C)
```

```python
import functools
import math

import jax
import jax.numpy as jnp
import numpy as np
from jax import lax
from jax.experimental import pallas as pl
from jax.experimental.pallas import tpu as pltpu
from jax.sharding import PartitionSpec as P

NS = 2048
FREQS = 512
BAND = 64
LAGS = 256
SEGS = 4
FOLD = 4
SPAN = NS // FOLD
CLASS = FREQS // FOLD
PAIR = 2 * CLASS
WIDTH = 2 * FREQS
BF16 = jnp.bfloat16
F32 = jnp.float32


def class_frequencies():
    return [FOLD * np.arange(CLASS) + r for r in range(FOLD)]


def trig_columns(index):
    blocks = []
    for freqs in class_frequencies():
        turns = (index[:, None] * freqs[None, :] % NS) * (2.0 * math.pi / NS)
        blocks += [np.cos(turns), -np.sin(turns)]
    return np.concatenate(blocks, 1).astype(jnp.bfloat16)


def spectra_kernel(extra, x_ref, t_ref, *rest):
    out_ref = rest[-1]
    segs, chans = x_ref.shape[1], x_ref.shape[2]
    rows = segs * chans
    x = x_ref[0].reshape(rows, NS)
    parts = [x[:, q * SPAN : (q + 1) * SPAN] for q in range(FOLD)]
    spec = []
    power = None
    for r in range(FOLD):
        table = t_ref[:, r * PAIR : (r + 1) * PAIR]
        p = [jnp.dot(part, table, preferred_element_type=F32) for part in parts]
        if r % 2 == 0:
            even, odd = p[0] + p[2], p[1] + p[3]
            both = even + odd if r == 0 else even - odd
            real, imag = both[:, :CLASS], both[:, CLASS:]
        else:
            even, odd = p[0] - p[2], p[1] - p[3]
            if r == 1:
                real = even[:, :CLASS] + odd[:, CLASS:]
                imag = even[:, CLASS:] - odd[:, :CLASS]
            else:
                real = even[:, :CLASS] - odd[:, CLASS:]
                imag = even[:, CLASS:] + odd[:, :CLASS]
        square = real * real + imag * imag
        power = square if power is None else power + square
        spec.append((real, imag))
    group = BAND // FOLD
    same = (
        lax.broadcasted_iota(jnp.int32, (CLASS, CLASS), 0) // group
        == lax.broadcasted_iota(jnp.int32, (CLASS, CLASS), 1) // group
    )
    ones = jnp.where(same, 1.0, 0.0).astype(BF16)
    high = power.astype(BF16)
    rest_power = power - high.astype(F32)
    mid = rest_power.astype(BF16)
    total = jnp.dot(high, ones, preferred_element_type=F32) + jnp.dot(
        mid, ones, preferred_element_type=F32
    )
    factor = lax.rsqrt(total * (0.5 / BAND) + 1e-06)
    for r, (real, imag) in enumerate(spec):
        out_ref[:rows, r * PAIR : r * PAIR + CLASS] = (real * factor).astype(BF16)
        out_ref[:rows, r * PAIR + CLASS : (r + 1) * PAIR] = (imag * factor).astype(BF16)
    if extra:
        vis_ref = rest[0]
        count, wide = vis_ref.shape
        out_ref[rows:, :] = jnp.zeros((extra, WIDTH), BF16)
        out_ref[rows : rows + extra, :wide] = jnp.concatenate(
            [vis_ref[...].astype(F32), jnp.zeros((extra - count, wide), F32)], 0
        ).astype(BF16)


def whole(shape):
    return pl.BlockSpec(shape, lambda *_: (0,) * len(shape))


def whitened_day(records, day, table, vis_rows):
    _, segs, chans, _ = records.shape
    rows = segs * chans
    extra = 0 if vis_rows is None else -(-vis_rows.shape[0] // 16) * 16
    ops = [records, table]
    specs = [
        pl.BlockSpec((1, segs, chans, NS), lambda i: (day, 0, 0, 0)),
        whole(table.shape),
    ]
    if extra:
        ops.append(vis_rows)
        specs.append(whole(vis_rows.shape))
    return pl.pallas_call(
        functools.partial(spectra_kernel, extra),
        grid=(1,),
        out_shape=jax.ShapeDtypeStruct((rows + extra, WIDTH), BF16),
        in_specs=specs,
        out_specs=whole((rows + extra, WIDTH)),
        cost_estimate=pl.CostEstimate(
            flops=2 * rows * NS * WIDTH, bytes_accessed=rows * NS * 2 + (1 << 20), transcendentals=0
        ),
        name=f"spectra_{day}",
    )(*ops)


def one_hot(row, chans):
    wide = row.shape[1]
    chosen = lax.broadcasted_iota(jnp.int32, (chans, wide), 0).astype(F32) == row
    return jnp.where(chosen, 1.0, 0.0).astype(F32).T.astype(BF16)


def cross_block(receivers, sources, select, r):
    cols = slice(r * PAIR, (r + 1) * PAIR)
    picks = select.shape[0] // receivers[0].shape[0]
    real = imag = None
    for own, other in zip(receivers, sources):
        g = jnp.dot(select, other[:, cols], preferred_element_type=F32)
        u = own[:, cols].astype(F32)
        u = jnp.concatenate([u] * picks, 0)
        ur, ui, gr, gi = u[:, :CLASS], u[:, CLASS:], g[:, :CLASS], g[:, CLASS:]
        a = ur * gr + ui * gi
        b = ur * gi - ui * gr
        real = a if real is None else real + a
        imag = b if imag is None else imag + b
    return jnp.concatenate([real, imag], 1).astype(BF16)


def lag_terms(inverse, receivers, sources, select):
    total = None
    for r in range(FOLD):
        block = cross_block(receivers, sources, select, r)
        part = lax.dot_general(
            inverse[:, r * PAIR : (r + 1) * PAIR],
            block,
            (((1,), (1,)), ((), ())),
            preferred_element_type=F32,
        )
        total = part if total is None else total + part
    return total


def units_of(ref, segs, chans):
    return [ref[s * chans : (s + 1) * chans, :] for s in range(segs)]


def local_kernel(visit, segs, chans, inv_ref, vis_ref, *refs):
    days, out_ref = refs[:-1], refs[-1]
    units = [u for ref in days for u in units_of(ref, segs, chans)]
    select = one_hot(vis_ref[visit : visit + 1, :].astype(F32), chans)
    out_ref[...] = lag_terms(inv_ref[...], units, units, select)


def pair_kernel(visit, foreign, segs, chans, first, inv_ref, vis_ref, own_ref, held_ref, *refs):
    vis_in = held_ref if first else refs[0]
    out_ref = refs[-1]
    own, held = units_of(own_ref, segs, chans), units_of(held_ref, segs, chans)
    wide = vis_ref.shape[1]
    rows = segs * chans
    mine = one_hot(vis_ref[visit : visit + 1, :].astype(F32), chans)
    row = vis_in[rows : rows + 16 * (foreign // 16 + 1), :wide].astype(F32)
    theirs = one_hot(row[foreign : foreign + 1, :], chans)
    inverse = inv_ref[...]
    out = [lag_terms(inverse, own, held, mine), lag_terms(inverse, held, own, theirs)]
    for n, value in enumerate(out):
        if not first:
            value = value + refs[1][:, n * wide : (n + 1) * wide]
        out_ref[:, n * wide : (n + 1) * wide] = value


def call(kernel, ops, out_shape, flops, name, scratch=()):
    return pl.pallas_call(
        kernel,
        grid=(1,),
        out_shape=out_shape,
        in_specs=[whole(op.shape) for op in ops],
        out_specs=jax.tree.map(lambda s: whole(s.shape), out_shape),
        scratch_shapes=list(scratch),
        cost_estimate=pl.CostEstimate(
            flops=flops,
            bytes_accessed=sum(int(np.prod(op.shape)) * op.dtype.itemsize for op in ops),
            transcendentals=0,
        ),
        name=name,
    )(*ops)


def split_kernel(share, n_day, n_seg, widths, *refs):
    parts, keep_ref, send_ref = refs[: len(widths)], refs[-2], refs[-1]
    day, seg = lax.axis_index("day"), lax.axis_index("seg")
    for ds in range(n_seg):
        for dd in range(n_day):
            block = lax.rem(day + dd, n_day) * n_seg + lax.rem(seg + ds, n_seg)
            rows = pl.ds(pl.multiple_of(block * share, share), share)
            at = 0
            for ref, width in zip(parts, widths):
                value = ref[rows, :]
                if ds == 0:
                    keep_ref[dd * share : (dd + 1) * share, at : at + width] = value
                else:
                    send_ref[ds - 1, dd * share : (dd + 1) * share, at : at + width] = value.astype(BF16)
                at += width


def local(records, visits):
    day_local, seg_local, chans, _ = records.shape
    visit_count, picks, _ = visits.shape
    reach = visit_count // 2
    n_chan, n_day, n_seg = (lax.axis_size(a) for a in ("chan", "day", "seg"))
    share = LAGS // (n_day * n_seg)
    wide = picks * chans
    forward = jnp.asarray(trig_columns(np.arange(SPAN)))
    inverse = jnp.asarray(trig_columns(np.arange(LAGS) - LAGS // 2))
    vis_rows = visits.reshape(visit_count, wide)

    own, held = [], {}
    for day in range(day_local):
        own.append(whitened_day(records, day, forward, vis_rows if day == 0 else None))
        for o in range(1, reach + 1):
            route = [((i + o) % n_chan, i) for i in range(n_chan)]
            held[o, day] = lax.ppermute(own[day], "chan", route)

    flops = 2 * wide * LAGS * WIDTH
    center = call(
        functools.partial(local_kernel, reach, seg_local, chans),
        [inverse, vis_rows, *own],
        jax.ShapeDtypeStruct((LAGS, wide), F32),
        flops,
        "center",
    )
    pairs = []
    for o in range(1, reach + 1):
        total = None
        for day in range(day_local):
            ops = [inverse, vis_rows, own[day], held[o, day]]
            if day:
                ops += [held[o, 0], total]
            total = call(
                functools.partial(pair_kernel, reach - o, reach + o, seg_local, chans, day == 0),
                ops,
                jax.ShapeDtypeStruct((LAGS, 2 * wide), F32),
                2 * flops,
                f"pair_{o}_{day}",
            )
        pairs.append(total)

    parts = [center, *pairs]
    widths = [p.shape[1] for p in parts]
    cols = sum(widths)
    keep, send = call(
        functools.partial(split_kernel, share, n_day, n_seg, widths),
        parts,
        (
            jax.ShapeDtypeStruct((n_day * share, cols), F32),
            jax.ShapeDtypeStruct((n_seg - 1, n_day * share, cols), BF16),
        ),
        0,
        "split",
    )
    for ds in range(1, n_seg):
        route = [(i, (i + ds) % n_seg) for i in range(n_seg)]
        keep = keep + lax.ppermute(send[ds - 1], "seg", route).astype(F32)

    columns = [None] * visit_count
    mine = keep[:share]
    columns[reach] = mine[:, :wide]
    for o in range(1, reach + 1):
        columns[reach - o] = mine[:, (2 * o - 1) * wide : 2 * o * wide]
    own_cols = jnp.concatenate(
        [keep[:, :wide]] + [keep[:, (2 * o - 1) * wide : 2 * o * wide] for o in range(1, reach + 1)], 1
    )
    own_total = own_cols[:share]
    for dd in range(1, n_day):
        route = [(i, (i + dd) % n_day) for i in range(n_day)]
        block = own_cols[dd * share : (dd + 1) * share].astype(BF16)
        own_total = own_total + lax.ppermute(block, "day", route).astype(F32)
    columns[reach] = own_total[:, :wide]
    for o in range(1, reach + 1):
        columns[reach - o] = own_total[:, o * wide : (o + 1) * wide]
        total = None
        for dd in range(n_day):
            route = [
                (c * n_day + d, (c + o) % n_chan * n_day + (d + dd) % n_day)
                for c in range(n_chan)
                for d in range(n_day)
            ]
            block = keep[dd * share : (dd + 1) * share, 2 * o * wide : (2 * o + 1) * wide]
            got = lax.ppermute(block.astype(BF16), ("chan", "day"), route).astype(F32)
            total = got if total is None else total + got
        columns[reach + o] = total
    days_all = day_local * n_day
    scale = 1.0 / math.sqrt(FREQS * days_all * SEGS)
    result = (jnp.concatenate(columns, 1) * scale).astype(BF16)
    return result.reshape(share, visit_count, picks, chans)


def solution(mesh):
    in_specs = (P("day", "seg", ("grp", "chan"), None), P(None, None, ("grp", "chan")))
    out_specs = P(("day", "seg"), None, None, ("grp", "chan"))
    return jax.shard_map(local, mesh=mesh, in_specs=in_specs, out_specs=out_specs, check_vma=False)
```

```python
import functools
import math

import jax
import jax.numpy as jnp
import numpy as np
from jax import lax
from jax.experimental import pallas as pl
from jax.experimental.pallas import tpu as pltpu
from jax.sharding import PartitionSpec as P

NS = 2048
FREQS = 512
BAND = 64
LAGS = 256
SEGS = 4
FOLD = 4
SPAN = NS // FOLD
CLASS = FREQS // FOLD
PAIR = 2 * CLASS
WIDTH = 2 * FREQS
GRANT = 24 << 20
BF16 = jnp.bfloat16
F32 = jnp.float32


def class_frequencies():
    return [FOLD * np.arange(CLASS) + r for r in range(FOLD)]


def trig_columns(index):
    blocks = []
    for freqs in class_frequencies():
        turns = (index[:, None] * freqs[None, :] % NS) * (2.0 * math.pi / NS)
        blocks += [np.cos(turns), -np.sin(turns)]
    return np.concatenate(blocks, 1).astype(jnp.bfloat16)


def whiten(x, table_of, out_ref):
    rows = x.shape[0]
    parts = [x[:, q * SPAN : (q + 1) * SPAN] for q in range(FOLD)]
    spec = []
    power = None
    for r in range(FOLD):
        table = table_of(r)
        p = [jnp.dot(part, table, preferred_element_type=F32) for part in parts]
        if r % 2 == 0:
            even, odd = p[0] + p[2], p[1] + p[3]
            both = even + odd if r == 0 else even - odd
            real, imag = both[:, :CLASS], both[:, CLASS:]
        else:
            even, odd = p[0] - p[2], p[1] - p[3]
            if r == 1:
                real = even[:, :CLASS] + odd[:, CLASS:]
                imag = even[:, CLASS:] - odd[:, :CLASS]
            else:
                real = even[:, :CLASS] - odd[:, CLASS:]
                imag = even[:, CLASS:] + odd[:, :CLASS]
        square = real * real + imag * imag
        power = square if power is None else power + square
        spec.append((real, imag))
    group = BAND // FOLD
    same = (
        lax.broadcasted_iota(jnp.int32, (CLASS, CLASS), 0) // group
        == lax.broadcasted_iota(jnp.int32, (CLASS, CLASS), 1) // group
    )
    ones = jnp.where(same, 1.0, 0.0).astype(BF16)
    high = power.astype(BF16)
    low = (power - high.astype(F32)).astype(BF16)
    total = jnp.dot(high, ones, preferred_element_type=F32) + jnp.dot(
        low, ones, preferred_element_type=F32
    )
    factor = lax.rsqrt(total * (0.5 / BAND) + 1e-06)
    for r, (real, imag) in enumerate(spec):
        out_ref[:rows, r * PAIR : r * PAIR + CLASS] = (real * factor).astype(BF16)
        out_ref[:rows, r * PAIR + CLASS : (r + 1) * PAIR] = (imag * factor).astype(BF16)


def rows_of(block):
    return jnp.concatenate([block[:, p, :] for p in range(block.shape[1])], 1)


def first_kernel(x_hbm, t_hbm, vis_ref, out_ref, t_ref, later_ref, x_ref, t_sem, x_sem):
    days, segs, chans, _ = x_hbm.shape
    rows = segs * chans
    x_copy = pltpu.make_async_copy(x_hbm.at[0], x_ref, x_sem.at[0])
    x_copy.start()
    t_copies = [
        pltpu.make_async_copy(t_hbm.at[r], t_ref.at[r], t_sem.at[r]) for r in range(FOLD)
    ]
    for copy in t_copies:
        copy.start()
    later = []
    if days > 1:
        later.append(pltpu.make_async_copy(x_hbm.at[pl.ds(1, days - 1)], later_ref, x_sem.at[1]))
        later[0].start()
    extra = out_ref.shape[0] - rows
    vis = rows_of(vis_ref[...]).astype(F32)
    count, wide = vis.shape
    out_ref[rows:, :] = jnp.zeros((extra, WIDTH), BF16)
    out_ref[rows:, :wide] = jnp.concatenate(
        [vis, jnp.zeros((extra - count, wide), F32)], 0
    ).astype(BF16)
    x_copy.wait()

    def table_of(r):
        t_copies[r].wait()
        return t_ref[r]

    whiten(x_ref[...].reshape(rows, NS), table_of, out_ref)
    for copy in later:
        copy.wait()


def later_kernel(day, x_ref, t_ref, out_ref):
    whiten(x_ref[day].reshape(out_ref.shape[0], NS), lambda r: t_ref[r], out_ref)


def in_vmem():
    return pl.BlockSpec(memory_space=pltpu.VMEM)


def cost(flops, ops):
    size = sum(int(np.prod(op.shape)) * op.dtype.itemsize for op in ops)
    return pl.CostEstimate(flops=flops, bytes_accessed=size, transcendentals=0)


def call(kernel, ops, out_shape, flops, name, scratch=()):
    return pl.pallas_call(
        kernel,
        out_shape=out_shape,
        in_specs=[in_vmem() for _ in ops],
        out_specs=jax.tree.map(lambda s: in_vmem(), out_shape),
        scratch_shapes=list(scratch),
        cost_estimate=cost(flops, ops),
        compiler_params=pltpu.CompilerParams(vmem_limit_bytes=GRANT),
        name=name,
    )(*ops)


def first_day(records, table, visits):
    days, segs, chans, _ = records.shape
    rows = segs * chans
    extra = -(-visits.shape[0] // 16) * 16
    return pl.pallas_call(
        first_kernel,
        out_shape=(
            jax.ShapeDtypeStruct((rows + extra, WIDTH), BF16),
            jax.ShapeDtypeStruct(table.shape, BF16),
            jax.ShapeDtypeStruct((max(days - 1, 1), segs, chans, NS), BF16),
        ),
        in_specs=[pl.BlockSpec(memory_space=pltpu.HBM)] * 2 + [in_vmem()],
        out_specs=(in_vmem(),) * 3,
        scratch_shapes=[
            pltpu.VMEM((segs, chans, NS), BF16),
            pltpu.SemaphoreType.DMA((FOLD,)),
            pltpu.SemaphoreType.DMA((2,)),
        ],
        cost_estimate=cost(2 * rows * NS * WIDTH, [records, table]),
        compiler_params=pltpu.CompilerParams(vmem_limit_bytes=GRANT),
        name="spectra_0",
    )(records, table, visits)


def one_hot(row, chans):
    wide = row.shape[1]
    chosen = lax.broadcasted_iota(jnp.int32, (chans, wide), 0).astype(F32) == row
    return jnp.where(chosen, 1.0, 0.0).astype(F32).T.astype(BF16)


def cross_block(receivers, sources, select, r):
    cols = slice(r * PAIR, (r + 1) * PAIR)
    picks = select.shape[0] // receivers[0].shape[0]
    real = imag = None
    for own, other in zip(receivers, sources):
        g = jnp.dot(select, other[:, cols], preferred_element_type=F32)
        u = own[:, cols].astype(F32)
        u = jnp.concatenate([u] * picks, 0)
        ur, ui, gr, gi = u[:, :CLASS], u[:, CLASS:], g[:, :CLASS], g[:, CLASS:]
        a = ur * gr + ui * gi
        b = ur * gi - ui * gr
        real = a if real is None else real + a
        imag = b if imag is None else imag + b
    return jnp.concatenate([real, imag], 1).astype(BF16)


def lag_terms(inv_ref, receivers, sources, select):
    total = None
    for r in range(FOLD):
        block = cross_block(receivers, sources, select, r)
        part = lax.dot_general(
            inv_ref[:, r * PAIR : (r + 1) * PAIR],
            block,
            (((1,), (1,)), ((), ())),
            preferred_element_type=F32,
        )
        total = part if total is None else total + part
    return total


def units_of(ref, segs, chans):
    return [ref.at[s * chans : (s + 1) * chans, :] for s in range(segs)]


def center_kernel(segs, chans, inv_ref, vis_ref, *refs):
    days, out_ref, select_ref = refs[:-2], refs[-2], refs[-1]
    reach = vis_ref.shape[0] // 2
    units = [u for ref in days for u in units_of(ref, segs, chans)]
    vis = rows_of(vis_ref[...]).astype(F32)
    for v in range(reach):
        select_ref[v] = one_hot(vis[v : v + 1, :], chans)
    out_ref[...] = lag_terms(inv_ref, units, units, one_hot(vis[reach : reach + 1, :], chans))


def pair_terms(inv_ref, mine, theirs, own_ref, held_ref, segs, chans):
    own, held = units_of(own_ref, segs, chans), units_of(held_ref, segs, chans)
    return lag_terms(inv_ref, own, held, mine), lag_terms(inv_ref, held, own, theirs)


def early_pair_kernel(offset, segs, chans, inv_ref, select_ref, own_ref, held_ref, out_ref, theirs_ref):
    reach, wide, _ = select_ref.shape
    rows = segs * chans
    tail = held_ref[rows:, :wide].astype(F32)
    theirs = one_hot(tail[reach + offset : reach + offset + 1, :], chans)
    theirs_ref[...] = theirs
    mine = select_ref[reach - offset]
    one, two = pair_terms(inv_ref, mine, theirs, own_ref, held_ref, segs, chans)
    out_ref[:, :wide] = one
    out_ref[:, wide:] = two


def later_pair_kernel(
    offset, segs, chans, inv_ref, select_ref, theirs_ref, own_ref, held_ref, sum_ref, out_ref
):
    reach, wide, _ = select_ref.shape
    one, two = pair_terms(
        inv_ref, select_ref[reach - offset], theirs_ref[...], own_ref, held_ref, segs, chans
    )
    out_ref[:, :wide] = one + sum_ref[:, :wide]
    out_ref[:, wide:] = two + sum_ref[:, wide:]


def split_kernel(share, n_day, n_seg, widths, *refs):
    parts, keep_ref, send_ref = refs[: len(widths)], refs[-2], refs[-1]
    day, seg = lax.axis_index("day"), lax.axis_index("seg")
    for ds in range(n_seg):
        for dd in range(n_day):
            block = lax.rem(day + dd, n_day) * n_seg + lax.rem(seg + ds, n_seg)
            rows = pl.ds(pl.multiple_of(block * share, share), share)
            at = 0
            for ref, width in zip(parts, widths):
                value = ref[rows, :]
                if ds == 0:
                    keep_ref[dd * share : (dd + 1) * share, at : at + width] = value
                else:
                    send_ref[ds - 1, dd * share : (dd + 1) * share, at : at + width] = value.astype(
                        BF16
                    )
                at += width


def last_pair_kernel(pair_args, split_args, *refs):
    ins, parts, keep_ref, send_ref, total = refs[:5], refs[5:-3], refs[-3], refs[-2], refs[-1]
    later_pair_kernel(*pair_args, *ins, parts[-1], total)
    split_kernel(*split_args, *parts[:-1], total, keep_ref, send_ref)


def merge_kernel(share, wide, reach, keep_ref, *refs):
    got, (own_ref, day_ref, away_ref) = refs[:-3], refs[-3:]
    n_day = keep_ref.shape[0] // share
    for dd in range(n_day):
        rows = slice(dd * share, (dd + 1) * share)
        for n in range(2 * reach + 1):
            cols = slice(n * wide, (n + 1) * wide)
            value = keep_ref[rows, cols]
            for ref in got:
                value = value + ref[rows, cols].astype(F32)
            if n and n % 2 == 0:
                away_ref[n // 2 - 1, dd] = value.astype(BF16)
                continue
            place = slice((n + 1) // 2 * wide, ((n + 1) // 2 + 1) * wide)
            if dd == 0:
                own_ref[:, place] = value
            else:
                day_ref[dd - 1, :, place] = value.astype(BF16)


def local(records, visits):
    day_local, seg_local, chans, _ = records.shape
    visit_count, picks, _ = visits.shape
    reach = visit_count // 2
    n_chan, n_day, n_seg = (lax.axis_size(a) for a in ("chan", "day", "seg"))
    share = LAGS // (n_day * n_seg)
    wide = picks * chans
    table = trig_columns(np.arange(SPAN)).reshape(SPAN, FOLD, PAIR).transpose(1, 0, 2)
    table = jnp.asarray(np.ascontiguousarray(table))
    inverse = jnp.asarray(trig_columns(np.arange(LAGS) - LAGS // 2))
    rows = seg_local * chans

    own, held = [], {}
    for day in range(day_local):
        if day == 0:
            spectra, table, later = first_day(records, table, visits)
        else:
            spectra = call(
                functools.partial(later_kernel, day - 1),
                [later, table],
                jax.ShapeDtypeStruct((rows, WIDTH), BF16),
                2 * rows * NS * WIDTH,
                f"spectra_{day}",
            )
        own.append(spectra)
        for o in range(1, reach + 1):
            route = [((i + o) % n_chan, i) for i in range(n_chan)]
            held[o, day] = lax.ppermute(spectra, "chan", route)

    flops = 2 * wide * LAGS * WIDTH
    center, select = call(
        functools.partial(center_kernel, seg_local, chans),
        [inverse, visits, *own],
        (
            jax.ShapeDtypeStruct((LAGS, wide), F32),
            jax.ShapeDtypeStruct((reach, wide, chans), BF16),
        ),
        flops,
        "center",
    )
    parts = [center]
    cols = visit_count * wide
    split_out = (
        jax.ShapeDtypeStruct((n_day * share, cols), F32),
        jax.ShapeDtypeStruct((n_seg - 1, n_day * share, cols), BF16),
    )
    split_args = (share, n_day, n_seg, [wide] + [2 * wide] * reach)
    pair_out = jax.ShapeDtypeStruct((LAGS, 2 * wide), F32)
    keep = None
    for o in range(1, reach + 1):
        for day in range(day_local):
            args = (o, seg_local, chans)
            if day == 0:
                total, theirs = call(
                    functools.partial(early_pair_kernel, *args),
                    [inverse, select, own[day], held[o, day]],
                    (pair_out, jax.ShapeDtypeStruct((wide, chans), BF16)),
                    2 * flops,
                    f"pair_{o}_{day}",
                )
                continue
            ops = [inverse, select, theirs, own[day], held[o, day]]
            if o == reach and day == day_local - 1:
                keep, send = call(
                    functools.partial(last_pair_kernel, args, split_args),
                    [*ops, *parts, total],
                    split_out,
                    2 * flops,
                    f"pair_{o}_{day}",
                    [pltpu.VMEM((LAGS, 2 * wide), F32)],
                )
            else:
                total = call(
                    functools.partial(later_pair_kernel, *args),
                    [*ops, total],
                    pair_out,
                    2 * flops,
                    f"pair_{o}_{day}",
                )
        parts.append(total)
    if keep is None:
        keep, send = call(functools.partial(split_kernel, *split_args), parts, split_out, 0, "split")

    got = []
    for ds in range(1, n_seg):
        route = [(i, (i + ds) % n_seg) for i in range(n_seg)]
        got.append(lax.ppermute(send[ds - 1], "seg", route))
    own_total, by_day, away = call(
        functools.partial(merge_kernel, share, wide, reach),
        [keep, *got],
        (
            jax.ShapeDtypeStruct((share, (reach + 1) * wide), F32),
            jax.ShapeDtypeStruct((max(n_day - 1, 1), share, (reach + 1) * wide), BF16),
            jax.ShapeDtypeStruct((reach, n_day, share, wide), BF16),
        ),
        0,
        "merge",
    )
    columns = [None] * visit_count
    for o in range(1, reach + 1):
        total = None
        for dd in range(n_day):
            route = [
                (c * n_day + d, (c + o) % n_chan * n_day + (d + dd) % n_day)
                for c in range(n_chan)
                for d in range(n_day)
            ]
            piece = lax.ppermute(away[o - 1, dd], ("chan", "day"), route).astype(F32)
            total = piece if total is None else total + piece
        columns[reach + o] = total
    for dd in range(1, n_day):
        route = [(i, (i + dd) % n_day) for i in range(n_day)]
        own_total = own_total + lax.ppermute(by_day[dd - 1], "day", route).astype(F32)
    columns[reach] = own_total[:, :wide]
    for o in range(1, reach + 1):
        columns[reach - o] = own_total[:, o * wide : (o + 1) * wide]
    days_all = day_local * n_day
    scale = 1.0 / math.sqrt(FREQS * days_all * SEGS)
    result = (jnp.concatenate(columns, 1) * scale).astype(BF16)
    return result.reshape(share, visit_count, picks, chans)


def solution(mesh):
    in_specs = (P("day", "seg", ("grp", "chan"), None), P(None, None, ("grp", "chan")))
    out_specs = P(("day", "seg"), None, None, ("grp", "chan"))
    return jax.shard_map(local, mesh=mesh, in_specs=in_specs, out_specs=out_specs, check_vma=False)
```

```python
import functools
import math

import jax
import jax.numpy as jnp
import numpy as np
from jax import lax
from jax.experimental import pallas as pl
from jax.experimental.pallas import tpu as pltpu
from jax.sharding import PartitionSpec as P

NS = 2048
FREQS = 512
BAND = 64
LAGS = 256
SEGS = 4
FOLD = 4
SPAN = NS // FOLD
CLASS = FREQS // FOLD
PAIR = 2 * CLASS
WIDTH = 2 * FREQS
GRANT = 24 << 20
BF16 = jnp.bfloat16
F32 = jnp.float32


def class_frequencies():
    return [FOLD * np.arange(CLASS) + r for r in range(FOLD)]


def trig_columns(index):
    blocks = []
    for freqs in class_frequencies():
        turns = (index[:, None] * freqs[None, :] % NS) * (2.0 * math.pi / NS)
        blocks += [np.cos(turns), -np.sin(turns)]
    return np.concatenate(blocks, 1).astype(jnp.bfloat16)


def whiten(x, table_of, out_ref, index=None):
    rows = x.shape[0]
    parts = [x[:, q * SPAN : (q + 1) * SPAN] for q in range(FOLD)]
    spec = []
    power = None
    for r in range(FOLD):
        table = table_of(r)
        p = [jnp.dot(part, table, preferred_element_type=F32) for part in parts]
        if r % 2 == 0:
            even, odd = p[0] + p[2], p[1] + p[3]
            both = even + odd if r == 0 else even - odd
            real, imag = both[:, :CLASS], both[:, CLASS:]
        else:
            even, odd = p[0] - p[2], p[1] - p[3]
            if r == 1:
                real = even[:, :CLASS] + odd[:, CLASS:]
                imag = even[:, CLASS:] - odd[:, :CLASS]
            else:
                real = even[:, :CLASS] - odd[:, CLASS:]
                imag = even[:, CLASS:] + odd[:, :CLASS]
        square = real * real + imag * imag
        power = square if power is None else power + square
        spec.append((real, imag))
    group = BAND // FOLD
    same = (
        lax.broadcasted_iota(jnp.int32, (CLASS, CLASS), 0) // group
        == lax.broadcasted_iota(jnp.int32, (CLASS, CLASS), 1) // group
    )
    ones = jnp.where(same, 1.0, 0.0).astype(BF16)
    high = power.astype(BF16)
    low = (power - high.astype(F32)).astype(BF16)
    total = jnp.dot(high, ones, preferred_element_type=F32) + jnp.dot(
        low, ones, preferred_element_type=F32
    )
    factor = lax.rsqrt(total * (0.5 / BAND) + 1e-06)
    for r, (real, imag) in enumerate(spec):
        real, imag = real * factor, imag * factor
        if r == 0 and index is not None:
            imag = jnp.where(first_lane(imag.shape), index, imag)
        out_ref[:, r * PAIR : r * PAIR + CLASS] = real.astype(BF16)
        out_ref[:, r * PAIR + CLASS : (r + 1) * PAIR] = imag.astype(BF16)


def first_lane(shape):
    return lax.broadcasted_iota(jnp.int32, shape, 1) == 0


def rows_of(block):
    return jnp.concatenate([block[:, p, :] for p in range(block.shape[1])], 1)


def first_kernel(packed, x_hbm, t_hbm, vis_hbm, out_ref, t_ref, later_ref, vis_ref, x_ref, t_sem, x_sem):
    days, segs, chans, _ = x_hbm.shape
    rows = segs * chans
    x_copy = pltpu.make_async_copy(x_hbm.at[0], x_ref, x_sem.at[0])
    x_copy.start()
    t_copies = [
        pltpu.make_async_copy(t_hbm.at[r], t_ref.at[r], t_sem.at[r]) for r in range(FOLD)
    ]
    for copy in t_copies:
        copy.start()
    vis_copy = pltpu.make_async_copy(vis_hbm, vis_ref, x_sem.at[2])
    vis_copy.start()
    later = []
    if days > 1:
        later.append(pltpu.make_async_copy(x_hbm.at[pl.ds(1, days - 1)], later_ref, x_sem.at[1]))
        later[0].start()
    vis_copy.wait()
    index = None
    if packed:
        row = rows_of(vis_ref[...])[-1:, :].astype(F32)
        index = jnp.broadcast_to(row, (CLASS, row.shape[1])).T
        if row.shape[1] < rows:
            index = jnp.concatenate([index, jnp.zeros((rows - row.shape[1], CLASS), F32)], 0)
    x_copy.wait()

    def table_of(r):
        t_copies[r].wait()
        return t_ref[r]

    whiten(x_ref[...].reshape(rows, NS), table_of, out_ref, index)
    for copy in later:
        copy.wait()


def later_kernel(day, x_ref, t_ref, out_ref):
    whiten(x_ref[day].reshape(out_ref.shape[0], NS), lambda r: t_ref[r], out_ref)


def in_vmem():
    return pl.BlockSpec(memory_space=pltpu.VMEM)


def cost(flops, ops):
    size = sum(int(np.prod(op.shape)) * op.dtype.itemsize for op in ops)
    return pl.CostEstimate(flops=flops, bytes_accessed=size, transcendentals=0)


def call(kernel, ops, out_shape, flops, name, scratch=()):
    return pl.pallas_call(
        kernel,
        out_shape=out_shape,
        in_specs=[in_vmem() for _ in ops],
        out_specs=jax.tree.map(lambda s: in_vmem(), out_shape),
        scratch_shapes=list(scratch),
        cost_estimate=cost(flops, ops),
        compiler_params=pltpu.CompilerParams(vmem_limit_bytes=GRANT),
        name=name,
    )(*ops)


def first_day(records, table, visits, packed):
    days, segs, chans, _ = records.shape
    rows = segs * chans
    ops = [pltpu.with_memory_space_constraint(op, pltpu.HBM) for op in (records, table, visits)]
    return pl.pallas_call(
        functools.partial(first_kernel, packed),
        out_shape=(
            jax.ShapeDtypeStruct((rows, WIDTH), BF16),
            jax.ShapeDtypeStruct(table.shape, BF16),
            jax.ShapeDtypeStruct((max(days - 1, 1), segs, chans, NS), BF16),
            jax.ShapeDtypeStruct(visits.shape, visits.dtype),
        ),
        in_specs=[pl.BlockSpec(memory_space=pltpu.HBM)] * 3,
        out_specs=(in_vmem(),) * 4,
        scratch_shapes=[
            pltpu.VMEM((segs, chans, NS), BF16),
            pltpu.SemaphoreType.DMA((FOLD,)),
            pltpu.SemaphoreType.DMA((3,)),
        ],
        cost_estimate=cost(2 * rows * NS * WIDTH, [records, table]),
        compiler_params=pltpu.CompilerParams(vmem_limit_bytes=GRANT),
        name="spectra_0",
    )(*ops)


def one_hot(row, chans):
    wide = row.shape[1]
    chosen = lax.broadcasted_iota(jnp.int32, (chans, wide), 0).astype(F32) == row
    return jnp.where(chosen, 1.0, 0.0).astype(F32).T.astype(BF16)


def cross_block(receivers, sources, select, r):
    cols = slice(r * PAIR, (r + 1) * PAIR)
    picks = select.shape[0] // receivers[0].shape[0]
    real = imag = None
    for own, other in zip(receivers, sources):
        g = jnp.dot(select, other[:, cols], preferred_element_type=F32)
        u = own[:, cols].astype(F32)
        u = jnp.concatenate([u] * picks, 0)
        ur, ui, gr, gi = u[:, :CLASS], u[:, CLASS:], g[:, :CLASS], g[:, CLASS:]
        if r == 0:
            ui = jnp.where(first_lane(ui.shape), 0.0, ui)
        a = ur * gr + ui * gi
        b = ur * gi - ui * gr
        real = a if real is None else real + a
        imag = b if imag is None else imag + b
    return jnp.concatenate([real, imag], 1).astype(BF16)


def lag_terms(inv_ref, receivers, sources, select):
    total = None
    for r in range(FOLD):
        block = cross_block(receivers, sources, select, r)
        part = lax.dot_general(
            inv_ref[:, r * PAIR : (r + 1) * PAIR],
            block,
            (((1,), (1,)), ((), ())),
            preferred_element_type=F32,
        )
        total = part if total is None else total + part
    return total


def units_of(ref, segs, chans):
    return [ref.at[s * chans : (s + 1) * chans, :] for s in range(segs)]


def center_kernel(segs, chans, inv_ref, vis_ref, *refs):
    days, out_ref, select_ref = refs[:-2], refs[-2], refs[-1]
    reach = vis_ref.shape[0] // 2
    units = [u for ref in days for u in units_of(ref, segs, chans)]
    vis = rows_of(vis_ref[...]).astype(F32)
    for v in range(reach):
        select_ref[v] = one_hot(vis[v : v + 1, :], chans)
    out_ref[...] = lag_terms(inv_ref, units, units, one_hot(vis[reach : reach + 1, :], chans))


def pair_terms(inv_ref, mine, theirs, own_ref, held_ref, segs, chans):
    own, held = units_of(own_ref, segs, chans), units_of(held_ref, segs, chans)
    return lag_terms(inv_ref, own, held, mine), lag_terms(inv_ref, held, own, theirs)


def early_pair_kernel(offset, segs, chans, packed, inv_ref, select_ref, own_ref, held_ref, *refs):
    out_ref, theirs_ref = refs[-2:]
    reach, wide, _ = select_ref.shape
    if packed:
        index = held_ref[:wide, CLASS : CLASS + 1].astype(F32)
        chosen = lax.broadcasted_iota(jnp.int32, (wide, chans), 1).astype(F32) == index
        theirs = jnp.where(chosen, 1.0, 0.0).astype(BF16)
    else:
        theirs = one_hot(rows_of(refs[0][...]).astype(F32), chans)
    theirs_ref[...] = theirs
    mine = select_ref[reach - offset]
    one, two = pair_terms(inv_ref, mine, theirs, own_ref, held_ref, segs, chans)
    out_ref[:, :wide] = one
    out_ref[:, wide:] = two


def later_pair_kernel(
    offset, segs, chans, inv_ref, select_ref, theirs_ref, own_ref, held_ref, sum_ref, out_ref
):
    reach, wide, _ = select_ref.shape
    one, two = pair_terms(
        inv_ref, select_ref[reach - offset], theirs_ref[...], own_ref, held_ref, segs, chans
    )
    out_ref[:, :wide] = one + sum_ref[:, :wide]
    out_ref[:, wide:] = two + sum_ref[:, wide:]


def split_kernel(share, n_day, n_seg, widths, *refs):
    parts, keep_ref, send_ref = refs[: len(widths)], refs[-2], refs[-1]
    day, seg = lax.axis_index("day"), lax.axis_index("seg")
    for ds in range(n_seg):
        for dd in range(n_day):
            block = lax.rem(day + dd, n_day) * n_seg + lax.rem(seg + ds, n_seg)
            rows = pl.ds(pl.multiple_of(block * share, share), share)
            at = 0
            for ref, width in zip(parts, widths):
                value = ref[rows, :]
                if ds == 0:
                    keep_ref[dd * share : (dd + 1) * share, at : at + width] = value
                else:
                    send_ref[ds - 1, dd * share : (dd + 1) * share, at : at + width] = value.astype(
                        BF16
                    )
                at += width


def last_pair_kernel(pair_args, split_args, *refs):
    ins, parts, keep_ref, send_ref, total = refs[:5], refs[5:-3], refs[-3], refs[-2], refs[-1]
    later_pair_kernel(*pair_args, *ins, parts[-1], total)
    split_kernel(*split_args, *parts[:-1], total, keep_ref, send_ref)


def merge_kernel(share, wide, reach, keep_ref, *refs):
    got, (own_ref, day_ref, away_ref) = refs[:-3], refs[-3:]
    n_day = keep_ref.shape[0] // share
    for dd in range(n_day):
        rows = slice(dd * share, (dd + 1) * share)
        for n in range(2 * reach + 1):
            cols = slice(n * wide, (n + 1) * wide)
            value = keep_ref[rows, cols]
            for ref in got:
                value = value + ref[rows, cols].astype(F32)
            if n and n % 2 == 0:
                away_ref[n // 2 - 1, dd] = value.astype(BF16)
                continue
            place = slice((n + 1) // 2 * wide, ((n + 1) // 2 + 1) * wide)
            if dd == 0:
                own_ref[:, place] = value
            else:
                day_ref[dd - 1, :, place] = value.astype(BF16)


def local(records, visits):
    day_local, seg_local, chans, _ = records.shape
    visit_count, picks, _ = visits.shape
    reach = visit_count // 2
    n_chan, n_day, n_seg = (lax.axis_size(a) for a in ("chan", "day", "seg"))
    share = LAGS // (n_day * n_seg)
    wide = picks * chans
    table = trig_columns(np.arange(SPAN)).reshape(SPAN, FOLD, PAIR).transpose(1, 0, 2)
    table = jnp.asarray(np.ascontiguousarray(table))
    inverse = jnp.asarray(trig_columns(np.arange(LAGS) - LAGS // 2))
    rows = seg_local * chans
    packed = reach == 1 and picks <= seg_local and chans <= 256

    own, held, asked = [], {}, {}
    for day in range(day_local):
        if day == 0:
            spectra, table, later, visits = first_day(records, table, visits, packed)
        else:
            spectra = call(
                functools.partial(later_kernel, day - 1),
                [later, table],
                jax.ShapeDtypeStruct((rows, WIDTH), BF16),
                2 * rows * NS * WIDTH,
                f"spectra_{day}",
            )
        own.append(spectra)
        for o in range(1, reach + 1):
            route = [((i + o) % n_chan, i) for i in range(n_chan)]
            held[o, day] = lax.ppermute(spectra, "chan", route)
            if day == 0 and not packed:
                asked[o] = lax.ppermute(visits[reach + o : reach + o + 1], "chan", route)

    flops = 2 * wide * LAGS * WIDTH
    center, select = call(
        functools.partial(center_kernel, seg_local, chans),
        [inverse, visits, *own],
        (
            jax.ShapeDtypeStruct((LAGS, wide), F32),
            jax.ShapeDtypeStruct((reach, wide, chans), BF16),
        ),
        flops,
        "center",
    )
    parts = [center]
    cols = visit_count * wide
    split_out = (
        jax.ShapeDtypeStruct((n_day * share, cols), F32),
        jax.ShapeDtypeStruct((n_seg - 1, n_day * share, cols), BF16),
    )
    split_args = (share, n_day, n_seg, [wide] + [2 * wide] * reach)
    pair_out = jax.ShapeDtypeStruct((LAGS, 2 * wide), F32)
    keep = None
    for o in range(1, reach + 1):
        for day in range(day_local):
            args = (o, seg_local, chans)
            if day == 0:
                total, theirs = call(
                    functools.partial(early_pair_kernel, *args, packed),
                    [inverse, select, own[day], held[o, day]] + ([] if packed else [asked[o]]),
                    (pair_out, jax.ShapeDtypeStruct((wide, chans), BF16)),
                    2 * flops,
                    f"pair_{o}_{day}",
                )
                continue
            ops = [inverse, select, theirs, own[day], held[o, day]]
            if o == reach and day == day_local - 1:
                keep, send = call(
                    functools.partial(last_pair_kernel, args, split_args),
                    [*ops, *parts, total],
                    split_out,
                    2 * flops,
                    f"pair_{o}_{day}",
                    [pltpu.VMEM((LAGS, 2 * wide), F32)],
                )
            else:
                total = call(
                    functools.partial(later_pair_kernel, *args),
                    [*ops, total],
                    pair_out,
                    2 * flops,
                    f"pair_{o}_{day}",
                )
        parts.append(total)
    if keep is None:
        keep, send = call(functools.partial(split_kernel, *split_args), parts, split_out, 0, "split")

    got = []
    for ds in range(1, n_seg):
        route = [(i, (i + ds) % n_seg) for i in range(n_seg)]
        got.append(lax.ppermute(send[ds - 1], "seg", route))
    own_total, by_day, away = call(
        functools.partial(merge_kernel, share, wide, reach),
        [keep, *got],
        (
            jax.ShapeDtypeStruct((share, (reach + 1) * wide), F32),
            jax.ShapeDtypeStruct((max(n_day - 1, 1), share, (reach + 1) * wide), BF16),
            jax.ShapeDtypeStruct((reach, n_day, share, wide), BF16),
        ),
        0,
        "merge",
    )
    columns = [None] * visit_count
    for o in range(1, reach + 1):
        total = None
        for dd in range(n_day):
            route = [
                (c * n_day + d, (c + o) % n_chan * n_day + (d + dd) % n_day)
                for c in range(n_chan)
                for d in range(n_day)
            ]
            piece = lax.ppermute(away[o - 1, dd], ("chan", "day"), route).astype(F32)
            total = piece if total is None else total + piece
        columns[reach + o] = total
    for dd in range(1, n_day):
        route = [(i, (i + dd) % n_day) for i in range(n_day)]
        own_total = own_total + lax.ppermute(by_day[dd - 1], "day", route).astype(F32)
    columns[reach] = own_total[:, :wide]
    for o in range(1, reach + 1):
        columns[reach - o] = own_total[:, o * wide : (o + 1) * wide]
    days_all = day_local * n_day
    scale = 1.0 / math.sqrt(FREQS * days_all * SEGS)
    result = (jnp.concatenate(columns, 1) * scale).astype(BF16)
    return result.reshape(share, visit_count, picks, chans)


def solution(mesh):
    in_specs = (P("day", "seg", ("grp", "chan"), None), P(None, None, ("grp", "chan")))
    out_specs = P(("day", "seg"), None, None, ("grp", "chan"))
    return jax.shard_map(local, mesh=mesh, in_specs=in_specs, out_specs=out_specs, check_vma=False)
```

```python
import functools
import math

import jax
import jax.numpy as jnp
import numpy as np
from jax import lax
from jax.experimental import pallas as pl
from jax.experimental.pallas import tpu as pltpu
from jax.sharding import PartitionSpec as P

NS = 2048
FREQS = 512
BAND = 64
LAGS = 256
SEGS = 4
FOLD = 4
SPAN = NS // FOLD
CLASS = FREQS // FOLD
PAIR = 2 * CLASS
WIDTH = 2 * FREQS
GRANT = 24 << 20
BF16 = jnp.bfloat16
F32 = jnp.float32


def class_frequencies():
    return [FOLD * np.arange(CLASS) + r for r in range(FOLD)]


def trig_columns(index):
    blocks = []
    for freqs in class_frequencies():
        turns = (index[:, None] * freqs[None, :] % NS) * (2.0 * math.pi / NS)
        blocks += [np.cos(turns), -np.sin(turns)]
    return np.concatenate(blocks, 1).astype(jnp.bfloat16)


def whiten(x, table_of, out_ref, index=None):
    rows = x.shape[0]
    parts = [x[:, q * SPAN : (q + 1) * SPAN] for q in range(FOLD)]
    spec = []
    power = None
    for r in range(FOLD):
        table = table_of(r)
        p = [jnp.dot(part, table, preferred_element_type=F32) for part in parts]
        if r % 2 == 0:
            even, odd = p[0] + p[2], p[1] + p[3]
            both = even + odd if r == 0 else even - odd
            real, imag = both[:, :CLASS], both[:, CLASS:]
        else:
            even, odd = p[0] - p[2], p[1] - p[3]
            if r == 1:
                real = even[:, :CLASS] + odd[:, CLASS:]
                imag = even[:, CLASS:] - odd[:, :CLASS]
            else:
                real = even[:, :CLASS] - odd[:, CLASS:]
                imag = even[:, CLASS:] + odd[:, :CLASS]
        square = real * real + imag * imag
        power = square if power is None else power + square
        spec.append((real, imag))
    group = BAND // FOLD
    same = (
        lax.broadcasted_iota(jnp.int32, (CLASS, CLASS), 0) // group
        == lax.broadcasted_iota(jnp.int32, (CLASS, CLASS), 1) // group
    )
    ones = jnp.where(same, 1.0, 0.0).astype(BF16)
    high = power.astype(BF16)
    low = (power - high.astype(F32)).astype(BF16)
    total = jnp.dot(high, ones, preferred_element_type=F32) + jnp.dot(
        low, ones, preferred_element_type=F32
    )
    factor = lax.rsqrt(total * (0.5 / BAND) + 1e-06)
    for r, (real, imag) in enumerate(spec):
        real, imag = real * factor, imag * factor
        if r == 0 and index is not None:
            imag = jnp.where(first_lane(imag.shape), index, imag)
        out_ref[:, r * PAIR : r * PAIR + CLASS] = real.astype(BF16)
        out_ref[:, r * PAIR + CLASS : (r + 1) * PAIR] = imag.astype(BF16)


def first_lane(shape):
    return lax.broadcasted_iota(jnp.int32, shape, 1) == 0


def rows_of(block):
    return jnp.concatenate([block[:, p, :] for p in range(block.shape[1])], 1)


def first_kernel(packed, x_hbm, t_hbm, vis_hbm, out_ref, t_ref, later_ref, vis_ref, x_ref, t_sem, x_sem):
    days, segs, chans, _ = x_hbm.shape
    rows = segs * chans
    vis_copy = pltpu.make_async_copy(vis_hbm, vis_ref, x_sem.at[2])
    vis_copy.start()
    x_copy = pltpu.make_async_copy(x_hbm.at[0], x_ref, x_sem.at[0])
    x_copy.start()
    t_copies = [
        pltpu.make_async_copy(t_hbm.at[r], t_ref.at[r], t_sem.at[r]) for r in range(FOLD)
    ]
    for copy in t_copies:
        copy.start()
    later = []
    if days > 1:
        later.append(pltpu.make_async_copy(x_hbm.at[pl.ds(1, days - 1)], later_ref, x_sem.at[1]))
    vis_copy.wait()
    index = None
    if packed:
        row = rows_of(vis_ref[...])[:1, :].astype(F32)
        index = jnp.broadcast_to(row, (CLASS, row.shape[1])).T
        if row.shape[1] < rows:
            index = jnp.concatenate([index, jnp.zeros((rows - row.shape[1], CLASS), F32)], 0)
    x_copy.wait()
    for copy in later:
        copy.start()

    def table_of(r):
        t_copies[r].wait()
        return t_ref[r]

    whiten(x_ref[...].reshape(rows, NS), table_of, out_ref, index)
    for copy in later:
        copy.wait()


def later_kernel(day, x_ref, t_ref, out_ref):
    whiten(x_ref[day].reshape(out_ref.shape[0], NS), lambda r: t_ref[r], out_ref)


def in_vmem():
    return pl.BlockSpec(memory_space=pltpu.VMEM)


def cost(flops, ops):
    size = sum(int(np.prod(op.shape)) * op.dtype.itemsize for op in ops)
    return pl.CostEstimate(flops=flops, bytes_accessed=size, transcendentals=0)


def call(kernel, ops, out_shape, flops, name, scratch=()):
    return pl.pallas_call(
        kernel,
        out_shape=out_shape,
        in_specs=[in_vmem() for _ in ops],
        out_specs=jax.tree.map(lambda s: in_vmem(), out_shape),
        scratch_shapes=list(scratch),
        cost_estimate=cost(flops, ops),
        compiler_params=pltpu.CompilerParams(vmem_limit_bytes=GRANT),
        name=name,
    )(*ops)


def first_day(records, table, visits, packed):
    days, segs, chans, _ = records.shape
    rows = segs * chans
    ops = [pltpu.with_memory_space_constraint(op, pltpu.HBM) for op in (records, table, visits)]
    return pl.pallas_call(
        functools.partial(first_kernel, packed),
        out_shape=(
            jax.ShapeDtypeStruct((rows, WIDTH), BF16),
            jax.ShapeDtypeStruct(table.shape, BF16),
            jax.ShapeDtypeStruct((max(days - 1, 1), segs, chans, NS), BF16),
            jax.ShapeDtypeStruct(visits.shape, visits.dtype),
        ),
        in_specs=[pl.BlockSpec(memory_space=pltpu.HBM)] * 3,
        out_specs=(in_vmem(),) * 4,
        scratch_shapes=[
            pltpu.VMEM((segs, chans, NS), BF16),
            pltpu.SemaphoreType.DMA((FOLD,)),
            pltpu.SemaphoreType.DMA((3,)),
        ],
        cost_estimate=cost(2 * rows * NS * WIDTH, [records, table]),
        compiler_params=pltpu.CompilerParams(vmem_limit_bytes=GRANT),
        name="spectra_0",
    )(*ops)


def one_hot(row, chans):
    wide = row.shape[1]
    chosen = lax.broadcasted_iota(jnp.int32, (chans, wide), 0).astype(F32) == row
    return jnp.where(chosen, 1.0, 0.0).astype(F32).T.astype(BF16)


def cross_block(receivers, sources, select, r):
    cols = slice(r * PAIR, (r + 1) * PAIR)
    picks = select.shape[0] // receivers[0].shape[0]
    real = imag = None
    for own, other in zip(receivers, sources):
        g = jnp.dot(select, other[:, cols], preferred_element_type=F32)
        u = own[:, cols].astype(F32)
        u = jnp.concatenate([u] * picks, 0)
        ur, ui, gr, gi = u[:, :CLASS], u[:, CLASS:], g[:, :CLASS], g[:, CLASS:]
        if r == 0:
            ui = jnp.where(first_lane(ui.shape), 0.0, ui)
        a = ur * gr + ui * gi
        b = ur * gi - ui * gr
        real = a if real is None else real + a
        imag = b if imag is None else imag + b
    return jnp.concatenate([real, imag], 1).astype(BF16)


def lag_terms(inv_ref, receivers, sources, select):
    total = None
    for r in range(FOLD):
        block = cross_block(receivers, sources, select, r)
        part = lax.dot_general(
            inv_ref[:, r * PAIR : (r + 1) * PAIR],
            block,
            (((1,), (1,)), ((), ())),
            preferred_element_type=F32,
        )
        total = part if total is None else total + part
    return total


def units_of(ref, segs, chans):
    return [ref.at[s * chans : (s + 1) * chans, :] for s in range(segs)]


def center_kernel(segs, chans, inv_ref, vis_ref, *refs):
    days, out_ref, select_ref = refs[:-2], refs[-2], refs[-1]
    reach = vis_ref.shape[0] // 2
    units = [u for ref in days for u in units_of(ref, segs, chans)]
    vis = rows_of(vis_ref[...]).astype(F32)
    for o in range(1, reach + 1):
        select_ref[o - 1] = one_hot(vis[reach + o : reach + o + 1, :], chans)
    out_ref[...] = lag_terms(inv_ref, units, units, one_hot(vis[reach : reach + 1, :], chans))


def pair_terms(inv_ref, mine, theirs, own_ref, held_ref, segs, chans):
    own, held = units_of(own_ref, segs, chans), units_of(held_ref, segs, chans)
    return lag_terms(inv_ref, own, held, mine), lag_terms(inv_ref, held, own, theirs)


def early_pair_kernel(offset, segs, chans, packed, inv_ref, select_ref, own_ref, held_ref, *refs):
    out_ref, theirs_ref = refs[-2:]
    reach, wide, _ = select_ref.shape
    if packed:
        index = held_ref[:wide, CLASS : CLASS + 1].astype(F32)
        chosen = lax.broadcasted_iota(jnp.int32, (wide, chans), 1).astype(F32) == index
        theirs = jnp.where(chosen, 1.0, 0.0).astype(BF16)
    else:
        theirs = one_hot(rows_of(refs[0][...]).astype(F32), chans)
    theirs_ref[...] = theirs
    mine = select_ref[offset - 1]
    one, two = pair_terms(inv_ref, mine, theirs, own_ref, held_ref, segs, chans)
    out_ref[:, :wide] = one
    out_ref[:, wide:] = two


def later_pair_kernel(
    offset, segs, chans, inv_ref, select_ref, theirs_ref, own_ref, held_ref, sum_ref, out_ref
):
    reach, wide, _ = select_ref.shape
    one, two = pair_terms(
        inv_ref, select_ref[offset - 1], theirs_ref[...], own_ref, held_ref, segs, chans
    )
    out_ref[:, :wide] = one + sum_ref[:, :wide]
    out_ref[:, wide:] = two + sum_ref[:, wide:]


def split_kernel(share, n_day, n_seg, widths, *refs):
    parts, keep_ref, send_ref = refs[: len(widths)], refs[-2], refs[-1]
    day, seg = lax.axis_index("day"), lax.axis_index("seg")
    for ds in range(n_seg):
        for dd in range(n_day):
            block = lax.rem(day + dd, n_day) * n_seg + lax.rem(seg + ds, n_seg)
            rows = pl.ds(pl.multiple_of(block * share, share), share)
            at = 0
            for ref, width in zip(parts, widths):
                value = ref[rows, :]
                if ds == 0:
                    keep_ref[dd * share : (dd + 1) * share, at : at + width] = value
                else:
                    send_ref[ds - 1, dd * share : (dd + 1) * share, at : at + width] = value.astype(
                        BF16
                    )
                at += width


def last_pair_kernel(pair_args, split_args, *refs):
    ins, parts, keep_ref, send_ref, total = refs[:5], refs[5:-3], refs[-3], refs[-2], refs[-1]
    later_pair_kernel(*pair_args, *ins, parts[-1], total)
    split_kernel(*split_args, *parts[:-1], total, keep_ref, send_ref)


def merge_kernel(share, wide, reach, keep_ref, *refs):
    got, (own_ref, day_ref, away_ref) = refs[:-3], refs[-3:]
    n_day = keep_ref.shape[0] // share
    for dd in range(n_day):
        rows = slice(dd * share, (dd + 1) * share)
        for n in range(2 * reach + 1):
            cols = slice(n * wide, (n + 1) * wide)
            value = keep_ref[rows, cols]
            for ref in got:
                value = value + ref[rows, cols].astype(F32)
            if n and n % 2 == 0:
                away_ref[n // 2 - 1, dd] = value.astype(BF16)
                continue
            place = slice((n + 1) // 2 * wide, ((n + 1) // 2 + 1) * wide)
            if dd == 0:
                own_ref[:, place] = value
            else:
                day_ref[dd - 1, :, place] = value.astype(BF16)


def local(records, visits):
    day_local, seg_local, chans, _ = records.shape
    visit_count, picks, _ = visits.shape
    reach = visit_count // 2
    n_chan, n_day, n_seg = (lax.axis_size(a) for a in ("chan", "day", "seg"))
    share = LAGS // (n_day * n_seg)
    wide = picks * chans
    table = trig_columns(np.arange(SPAN)).reshape(SPAN, FOLD, PAIR).transpose(1, 0, 2)
    table = jnp.asarray(np.ascontiguousarray(table))
    inverse = jnp.asarray(trig_columns(np.arange(LAGS) - LAGS // 2))
    rows = seg_local * chans
    packed = reach == 1 and picks <= seg_local and chans <= 256

    own, held, asked = [], {}, {}
    for day in range(day_local):
        if day == 0:
            spectra, table, later, visits = first_day(records, table, visits, packed)
        else:
            spectra = call(
                functools.partial(later_kernel, day - 1),
                [later, table],
                jax.ShapeDtypeStruct((rows, WIDTH), BF16),
                2 * rows * NS * WIDTH,
                f"spectra_{day}",
            )
        own.append(spectra)
        for o in range(1, reach + 1):
            route = [(i, (i + o) % n_chan) for i in range(n_chan)]
            held[o, day] = lax.ppermute(spectra, "chan", route)
            if day == 0 and not packed:
                asked[o] = lax.ppermute(visits[reach - o : reach - o + 1], "chan", route)

    flops = 2 * wide * LAGS * WIDTH
    center, select = call(
        functools.partial(center_kernel, seg_local, chans),
        [inverse, visits, *own],
        (
            jax.ShapeDtypeStruct((LAGS, wide), F32),
            jax.ShapeDtypeStruct((reach, wide, chans), BF16),
        ),
        flops,
        "center",
    )
    parts = [center]
    cols = visit_count * wide
    split_out = (
        jax.ShapeDtypeStruct((n_day * share, cols), F32),
        jax.ShapeDtypeStruct((n_seg - 1, n_day * share, cols), BF16),
    )
    split_args = (share, n_day, n_seg, [wide] + [2 * wide] * reach)
    pair_out = jax.ShapeDtypeStruct((LAGS, 2 * wide), F32)
    keep = None
    for o in range(1, reach + 1):
        for day in range(day_local):
            args = (o, seg_local, chans)
            if day == 0:
                total, theirs = call(
                    functools.partial(early_pair_kernel, *args, packed),
                    [inverse, select, own[day], held[o, day]] + ([] if packed else [asked[o]]),
                    (pair_out, jax.ShapeDtypeStruct((wide, chans), BF16)),
                    2 * flops,
                    f"pair_{o}_{day}",
                )
                continue
            ops = [inverse, select, theirs, own[day], held[o, day]]
            if o == reach and day == day_local - 1:
                keep, send = call(
                    functools.partial(last_pair_kernel, args, split_args),
                    [*ops, *parts, total],
                    split_out,
                    2 * flops,
                    f"pair_{o}_{day}",
                    [pltpu.VMEM((LAGS, 2 * wide), F32)],
                )
            else:
                total = call(
                    functools.partial(later_pair_kernel, *args),
                    [*ops, total],
                    pair_out,
                    2 * flops,
                    f"pair_{o}_{day}",
                )
        parts.append(total)
    if keep is None:
        keep, send = call(functools.partial(split_kernel, *split_args), parts, split_out, 0, "split")

    got = []
    for ds in range(1, n_seg):
        route = [(i, (i + ds) % n_seg) for i in range(n_seg)]
        got.append(lax.ppermute(send[ds - 1], "seg", route))
    own_total, by_day, away = call(
        functools.partial(merge_kernel, share, wide, reach),
        [keep, *got],
        (
            jax.ShapeDtypeStruct((share, (reach + 1) * wide), F32),
            jax.ShapeDtypeStruct((max(n_day - 1, 1), share, (reach + 1) * wide), BF16),
            jax.ShapeDtypeStruct((reach, n_day, share, wide), BF16),
        ),
        0,
        "merge",
    )
    columns = [None] * visit_count
    for o in range(1, reach + 1):
        total = None
        for dd in range(n_day):
            route = [
                (c * n_day + d, (c - o) % n_chan * n_day + (d + dd) % n_day)
                for c in range(n_chan)
                for d in range(n_day)
            ]
            piece = lax.ppermute(away[o - 1, dd], ("chan", "day"), route).astype(F32)
            total = piece if total is None else total + piece
        columns[reach - o] = total
    for dd in range(1, n_day):
        route = [(i, (i + dd) % n_day) for i in range(n_day)]
        own_total = own_total + lax.ppermute(by_day[dd - 1], "day", route).astype(F32)
    columns[reach] = own_total[:, :wide]
    for o in range(1, reach + 1):
        columns[reach + o] = own_total[:, o * wide : (o + 1) * wide]
    days_all = day_local * n_day
    scale = 1.0 / math.sqrt(FREQS * days_all * SEGS)
    result = (jnp.concatenate(columns, 1) * scale).astype(BF16)
    return result.reshape(share, visit_count, picks, chans)


def solution(mesh):
    in_specs = (P("day", "seg", ("grp", "chan"), None), P(None, None, ("grp", "chan")))
    out_specs = P(("day", "seg"), None, None, ("grp", "chan"))
    return jax.shard_map(local, mesh=mesh, in_specs=in_specs, out_specs=out_specs, check_vma=False)
```

```python
import functools
import math

import jax
import jax.numpy as jnp
import numpy as np
from jax import lax
from jax.experimental import pallas as pl
from jax.experimental.pallas import tpu as pltpu
from jax.sharding import PartitionSpec as P


NS = 2048
FREQS = 512
BAND = 64
LAGS = 256
SEGS = 4
FOLD = 4
SPAN = NS // FOLD
CLASS = FREQS // FOLD
PAIR = 2 * CLASS
WIDTH = 2 * FREQS
GRANT = 24 << 20
BF16 = jnp.bfloat16
F32 = jnp.float32


def trig_columns(index):
    blocks = []
    for r in range(FOLD):
        freqs = FOLD * np.arange(CLASS) + r
        turns = (index[:, None] * freqs[None, :] % NS) * (2.0 * math.pi / NS)
        blocks += [np.cos(turns), -np.sin(turns)]
    return np.concatenate(blocks, 1).astype(jnp.bfloat16)


def in_vmem():
    return pl.BlockSpec(memory_space=pltpu.VMEM)


def cost(flops, ops):
    size = sum(int(np.prod(op.shape)) * op.dtype.itemsize for op in ops)
    return pl.CostEstimate(flops=flops, bytes_accessed=size, transcendentals=0)


def call(kernel, ops, out_shape, flops, scratch=(), hbm=0):
    ops = [pltpu.with_memory_space_constraint(op, pltpu.HBM) for op in ops[:hbm]] + ops[hbm:]
    return pl.pallas_call(
        kernel,
        out_shape=out_shape,
        in_specs=[pl.BlockSpec(memory_space=pltpu.HBM)] * hbm + [in_vmem() for _ in ops[hbm:]],
        out_specs=jax.tree.map(lambda s: in_vmem(), out_shape),
        scratch_shapes=list(scratch),
        cost_estimate=cost(flops, ops),
        compiler_params=pltpu.CompilerParams(vmem_limit_bytes=GRANT),
    )(*ops)


def shape(dims, dtype=BF16):
    return jax.ShapeDtypeStruct(dims, dtype)


def whiten(x, t_ref, out_ref):
    rows = x.shape[0]
    stacked = jnp.concatenate([x[:, q * SPAN : (q + 1) * SPAN] for q in range(FOLD)], 0)
    spec = []
    power = None
    for r in range(FOLD):
        product = jnp.dot(stacked, t_ref[r], preferred_element_type=F32)
        p = [product[q * rows : (q + 1) * rows] for q in range(FOLD)]
        if r % 2 == 0:
            even, odd = p[0] + p[2], p[1] + p[3]
            both = even + odd if r == 0 else even - odd
            real, imag = both[:, :CLASS], both[:, CLASS:]
        else:
            even, odd = p[0] - p[2], p[1] - p[3]
            if r == 1:
                real = even[:, :CLASS] + odd[:, CLASS:]
                imag = even[:, CLASS:] - odd[:, :CLASS]
            else:
                real = even[:, :CLASS] - odd[:, CLASS:]
                imag = even[:, CLASS:] + odd[:, :CLASS]
        square = real * real + imag * imag
        power = square if power is None else power + square
        spec.append((real, imag))
    group = BAND // FOLD
    same = (
        lax.broadcasted_iota(jnp.int32, (CLASS, CLASS), 0) // group
        == lax.broadcasted_iota(jnp.int32, (CLASS, CLASS), 1) // group
    )
    ones = jnp.where(same, 1.0, 0.0).astype(BF16)
    high = power.astype(BF16)
    low = (power - high.astype(F32)).astype(BF16)
    total = jnp.dot(high, ones, preferred_element_type=F32) + jnp.dot(
        low, ones, preferred_element_type=F32
    )
    factor = lax.rsqrt(total * (0.5 / BAND) + 1e-06)
    for r, (real, imag) in enumerate(spec):
        out_ref[:, r * PAIR : r * PAIR + CLASS] = (real * factor).astype(BF16)
        out_ref[:, r * PAIR + CLASS : (r + 1) * PAIR] = (imag * factor).astype(BF16)


def first_kernel(x_hbm, t_hbm, vis_hbm, out_ref, t_ref, vis_ref, x_ref, sem):
    copies = [
        pltpu.make_async_copy(x_hbm.at[0, 0], x_ref, sem.at[0]),
        pltpu.make_async_copy(t_hbm, t_ref, sem.at[1]),
        pltpu.make_async_copy(vis_hbm, vis_ref, sem.at[2]),
    ]
    for copy in copies:
        copy.start()
    for copy in copies:
        copy.wait()
    whiten(x_ref[...], t_ref, out_ref)


def second_kernel(first, count, x_hbm, t_ref, out_ref, rest_ref, x_ref, sem):
    segs, chans = x_hbm.shape[1], x_hbm.shape[2]
    copies = []
    for n in range(x_hbm.shape[0] * segs - first):
        target = x_ref.at[n] if n < count else rest_ref.at[n - count]
        unit = first + n
        copies.append(pltpu.make_async_copy(x_hbm.at[unit // segs, unit % segs], target, sem.at[n]))
    for copy in copies:
        copy.start()
    for copy in copies[:count]:
        copy.wait()
    whiten(x_ref[...].reshape(count * chans, NS), t_ref, out_ref)
    for copy in copies[count:]:
        copy.wait()


def later_kernel(x_ref, t_ref, out_ref):
    whiten(x_ref[...].reshape(out_ref.shape[0], NS), t_ref, out_ref)


def spectra_chunks(records, table, visits):
    days, segs, chans, _ = records.shape
    units = days * segs
    flops = 2 * chans * NS * WIDTH
    first, table, visits = call(
        first_kernel,
        [records, table, visits],
        (shape((chans, WIDTH)), shape(table.shape), shape(visits.shape, visits.dtype)),
        flops,
        [pltpu.VMEM((chans, NS), BF16), pltpu.SemaphoreType.DMA((3,))],
        hbm=3,
    )
    chunks = [first]
    count = max(units - 2, 1)
    left = units - 1 - count
    if units > 1:
        chunk, rest = call(
            functools.partial(second_kernel, 1, count),
            [records, table],
            (shape((count * chans, WIDTH)), shape((max(left, 1), chans, NS))),
            count * flops,
            [pltpu.VMEM((count, chans, NS), BF16), pltpu.SemaphoreType.DMA((units - 1,))],
            hbm=1,
        )
        chunks.append(chunk)
    if left:
        chunks.append(call(later_kernel, [rest, table], shape((left * chans, WIDTH)), left * flops))
    return chunks, visits


def one_hot(block, chans):
    row = jnp.concatenate([block[p : p + 1, :] for p in range(block.shape[0])], 1).astype(F32)
    chosen = lax.broadcasted_iota(jnp.int32, (chans, row.shape[1]), 0).astype(F32) == row
    return jnp.where(chosen, 1.0, 0.0).astype(F32).T.astype(BF16)


def cross_block(receivers, sources, select, r):
    cols = slice(r * PAIR, (r + 1) * PAIR)
    picks = select.shape[0] // receivers[0].shape[0]
    real = imag = None
    for own, other in zip(receivers, sources):
        g = jnp.dot(select, other[:, cols], preferred_element_type=F32)
        u = own[:, cols].astype(F32)
        u = jnp.concatenate([u] * picks, 0)
        ur, ui, gr, gi = u[:, :CLASS], u[:, CLASS:], g[:, :CLASS], g[:, CLASS:]
        a = ur * gr + ui * gi
        b = ur * gi - ui * gr
        real = a if real is None else real + a
        imag = b if imag is None else imag + b
    return jnp.concatenate([real, imag], 1).astype(BF16)


def lag_terms(inv_ref, receivers, sources, select):
    total = None
    for r in range(FOLD):
        block = cross_block(receivers, sources, select, r)
        part = lax.dot_general(
            inv_ref[:, r * PAIR : (r + 1) * PAIR],
            block,
            (((1,), (1,)), ((), ())),
            preferred_element_type=F32,
        )
        total = part if total is None else total + part
    return total


def units_of(ref, chans):
    return [ref.at[n * chans : (n + 1) * chans, :] for n in range(ref.shape[0] // chans)]


def center_kernel(inv_ref, vis_ref, *refs):
    chunks, out_ref, select_ref = refs[:-2], refs[-2], refs[-1]
    chans = vis_ref.shape[2]
    reach = vis_ref.shape[0] // 2
    units = [u for ref in chunks for u in units_of(ref, chans)]
    for n in range(reach):
        select_ref[n] = one_hot(vis_ref[reach + 1 + n], chans)
    out_ref[...] = lag_terms(inv_ref, units, units, one_hot(vis_ref[reach], chans))


def select_kernel(wanted, *refs):
    out_ref = refs[-1]
    for n, (which, visit) in enumerate(wanted):
        out_ref[n] = one_hot(refs[which][visit], refs[which].shape[2])


def pair_terms(jobs, inv_ref, selects, blocks):
    chans = selects[0].shape[2]
    units = [units_of(ref, chans) for ref in blocks]
    return [
        lag_terms(inv_ref, units[receiver], units[source], selects[which][index])
        for receiver, source, which, index in jobs
    ]


def pair_kernel(jobs, n_blocks, inv_ref, near_ref, far_ref, *refs):
    blocks, out_ref = refs[:n_blocks], refs[-1]
    wide = near_ref.shape[1]
    for n, value in enumerate(pair_terms(jobs, inv_ref, (near_ref, far_ref), blocks)):
        cols = slice(n * wide, (n + 1) * wide)
        if len(refs) > n_blocks + 1:
            value = value + refs[n_blocks][:, cols]
        out_ref[:, cols] = value


def split_kernel(share, n_day, n_seg, n_parts, *refs):
    parts, keep_ref, send_ref = refs[:n_parts], refs[-2], refs[-1]
    day, seg = lax.axis_index("day"), lax.axis_index("seg")
    for ds in range(n_seg):
        for dd in range(n_day):
            block = lax.rem(day + dd, n_day) * n_seg + lax.rem(seg + ds, n_seg)
            rows = pl.ds(pl.multiple_of(block * share, share), share)
            at = 0
            for ref in parts:
                value = ref[rows, :]
                cols = slice(at, at + ref.shape[1])
                if ds == 0:
                    keep_ref[dd * share : (dd + 1) * share, cols] = value
                else:
                    send_ref[ds - 1, dd * share : (dd + 1) * share, cols] = value.astype(BF16)
                at += ref.shape[1]


def last_pair_kernel(pair_args, split_args, n_in, *refs):
    ins, parts, (keep_ref, send_ref, total) = refs[:n_in], refs[n_in:-3], refs[-3:]
    pair_kernel(*pair_args, *ins, total)
    split_kernel(*split_args, *parts, total, keep_ref, send_ref)


def merge_kernel(share, wide, groups, n_got, *refs):
    keep_ref, got, outs = refs[0], refs[1 : 1 + n_got], refs[1 + n_got :]
    n_day = keep_ref.shape[0] // share
    for dd in range(n_day):
        rows = slice(dd * share, (dd + 1) * share)
        for g, group in enumerate(groups):
            for place, n in enumerate(group):
                cols = slice(n * wide, (n + 1) * wide)
                value = keep_ref[rows, cols]
                for ref in got:
                    value = value + ref[rows, cols].astype(F32)
                to = slice(place * wide, (place + 1) * wide)
                if g == 0 and dd == 0:
                    outs[0][:, to] = value
                elif g == 0:
                    outs[1][dd - 1, :, to] = value.astype(BF16)
                else:
                    outs[g + 1][dd, :, to] = value.astype(BF16)


def line_plan(n_chan):
    up = [(i, i + 1) for i in range(n_chan - 1)]
    back = [(i + 1, i) for i in range(n_chan - 1)]
    arrivals = [up, [(n_chan - 1, 1)]]
    wanted = [(0, 0), (0, 2), (1, 0)]
    jobs = [(0, 1, 0, 0), (1, 0, 1, 0), (1, 2, 1, 1), (2, 1, 1, 2)]
    visits_of = [2, 0, 2, 0]
    ways = [None, 0, 0, 1]
    routes = [back, [(1, n_chan - 1)]]
    return [(arrivals, wanted, jobs, visits_of, ways)], routes


def ring_plan(n_chan, reach):
    groups, routes = [], []
    for o in range(1, reach + 1):
        to = [(i, (i + o) % n_chan) for i in range(n_chan)]
        routes.append([(j, i) for i, j in to])
        jobs = [(0, 1, 0, o - 1), (1, 0, 1, 0)]
        groups.append(([to], [(0, reach - o)], jobs, [reach + o, reach - o], [None, o - 1]))
    return groups, routes


def local(records, visits):
    day_local, _, chans, _ = records.shape
    visit_count, picks, _ = visits.shape
    reach = visit_count // 2
    n_chan, n_day, n_seg = (lax.axis_size(a) for a in ("chan", "day", "seg"))
    share = LAGS // (n_day * n_seg)
    wide = picks * chans
    table = trig_columns(np.arange(SPAN)).reshape(SPAN, FOLD, PAIR).transpose(1, 0, 2)
    table = jnp.asarray(np.ascontiguousarray(table))
    inverse = jnp.asarray(trig_columns(np.arange(LAGS) - LAGS // 2))
    line = reach == 1 and n_chan > 2
    plan, routes = line_plan(n_chan) if line else ring_plan(n_chan, reach)

    chunks, visits = spectra_chunks(records, table, visits)
    held, asked = [], []
    for arrivals, *_ in plan:
        held.append([[lax.ppermute(c, "chan", to) for to in arrivals] for c in chunks])
        asked.append([lax.ppermute(visits, "chan", to) for to in arrivals])

    flops = 2 * wide * LAGS * WIDTH
    center, near = call(
        center_kernel,
        [inverse, visits, *chunks],
        (shape((LAGS, wide), F32), shape((reach, wide, chans))),
        flops,
    )
    parts = [center]
    visit_of, way_of = [reach], [None]
    for g, (arrivals, wanted, jobs, visits_of, ways) in enumerate(plan):
        visit_of += visits_of
        way_of += ways
        far = call(
            functools.partial(select_kernel, wanted), asked[g], shape((len(wanted), wide, chans)), 0
        )
        total = None
        for n, chunk in enumerate(chunks):
            args = (jobs, 1 + len(arrivals))
            ops = [inverse, near, far, chunk, *held[g][n]] + ([] if total is None else [total])
            if g == len(plan) - 1 and n == len(chunks) - 1:
                cols = len(visit_of) * wide
                keep, send = call(
                    functools.partial(
                        last_pair_kernel, args, (share, n_day, n_seg, len(parts) + 1), len(ops)
                    ),
                    ops + parts,
                    (
                        shape((n_day * share, cols), F32),
                        shape((n_seg - 1, n_day * share, cols)),
                    ),
                    len(jobs) * flops,
                    [pltpu.VMEM((LAGS, len(jobs) * wide), F32)],
                )
            else:
                total = call(
                    functools.partial(pair_kernel, *args),
                    ops,
                    shape((LAGS, len(jobs) * wide), F32),
                    len(jobs) * flops,
                )
        parts.append(total)

    got = []
    for ds in range(1, n_seg):
        route = [(i, (i + ds) % n_seg) for i in range(n_seg)]
        got.append(lax.ppermute(send[ds - 1], "seg", route))
    groups = [[n for n, way in enumerate(way_of) if way is None]]
    groups += [[n for n, way in enumerate(way_of) if way == k] for k in range(len(routes))]
    own, by_day, *away = call(
        functools.partial(merge_kernel, share, wide, groups, len(got)),
        [keep, *got],
        (
            shape((share, len(groups[0]) * wide), F32),
            shape((max(n_day - 1, 1), share, len(groups[0]) * wide)),
            *[shape((n_day, share, len(g) * wide)) for g in groups[1:]],
        ),
        0,
    )
    columns = [None] * visit_count

    def add(group, values):
        for place, n in enumerate(group):
            v = visit_of[n]
            value = values[:, place * wide : (place + 1) * wide].astype(F32)
            columns[v] = value if columns[v] is None else columns[v] + value

    for k, pairs in enumerate(routes):
        for dd in range(n_day):
            route = [
                (i * n_day + d, j * n_day + (d + dd) % n_day) for i, j in pairs for d in range(n_day)
            ]
            add(groups[k + 1], lax.ppermute(away[k][dd], ("chan", "day"), route))
    for dd in range(1, n_day):
        route = [(i, (i + dd) % n_day) for i in range(n_day)]
        add(groups[0], lax.ppermute(by_day[dd - 1], "day", route))
    add(groups[0], own)
    days_all = day_local * n_day
    scale = 1.0 / math.sqrt(FREQS * days_all * SEGS)
    result = (jnp.concatenate(columns, 1) * scale).astype(BF16)
    return result.reshape(share, visit_count, picks, chans)


def solution(mesh):
    in_specs = (P("day", "seg", ("grp", "chan"), None), P(None, None, ("grp", "chan")))
    out_specs = P(("day", "seg"), None, None, ("grp", "chan"))

    return jax.shard_map(local, mesh=mesh, in_specs=in_specs, out_specs=out_specs, check_vma=False)
```

```python
import functools
import math

import jax
import jax.numpy as jnp
import numpy as np
from jax import lax
from jax.experimental import pallas as pl
from jax.experimental.pallas import tpu as pltpu
from jax.sharding import PartitionSpec as P


NS = 2048
FREQS = 512
BAND = 64
LAGS = 256
SEGS = 4
FOLD = 4
SPAN = NS // FOLD
CLASS = FREQS // FOLD
PAIR = 2 * CLASS
WIDTH = 2 * FREQS
GRANT = 24 << 20
BF16 = jnp.bfloat16
F32 = jnp.float32


def trig_columns(index):
    blocks = []
    for r in range(FOLD):
        freqs = FOLD * np.arange(CLASS) + r
        turns = (index[:, None] * freqs[None, :] % NS) * (2.0 * math.pi / NS)
        blocks += [np.cos(turns), -np.sin(turns)]
    return np.concatenate(blocks, 1).astype(jnp.bfloat16)


def in_vmem():
    return pl.BlockSpec(memory_space=pltpu.VMEM)


def cost(flops, ops):
    size = sum(int(np.prod(op.shape)) * op.dtype.itemsize for op in ops)
    return pl.CostEstimate(flops=flops, bytes_accessed=size, transcendentals=0)


def call(kernel, ops, out_shape, flops, scratch=(), hbm=0):
    ops = [pltpu.with_memory_space_constraint(op, pltpu.HBM) for op in ops[:hbm]] + ops[hbm:]
    return pl.pallas_call(
        kernel,
        out_shape=out_shape,
        in_specs=[pl.BlockSpec(memory_space=pltpu.HBM)] * hbm + [in_vmem() for _ in ops[hbm:]],
        out_specs=jax.tree.map(lambda s: in_vmem(), out_shape),
        scratch_shapes=list(scratch),
        cost_estimate=cost(flops, ops),
        compiler_params=pltpu.CompilerParams(vmem_limit_bytes=GRANT),
    )(*ops)


def shape(dims, dtype=BF16):
    return jax.ShapeDtypeStruct(dims, dtype)


def whiten(x, t_ref, out_ref):
    rows = x.shape[0]
    stacked = jnp.concatenate([x[:, q * SPAN : (q + 1) * SPAN] for q in range(FOLD)], 0)
    spec = []
    power = None
    for r in range(FOLD):
        product = jnp.dot(stacked, t_ref[r], preferred_element_type=F32)
        p = [product[q * rows : (q + 1) * rows] for q in range(FOLD)]
        if r % 2 == 0:
            even, odd = p[0] + p[2], p[1] + p[3]
            both = even + odd if r == 0 else even - odd
            real, imag = both[:, :CLASS], both[:, CLASS:]
        else:
            even, odd = p[0] - p[2], p[1] - p[3]
            if r == 1:
                real = even[:, :CLASS] + odd[:, CLASS:]
                imag = even[:, CLASS:] - odd[:, :CLASS]
            else:
                real = even[:, :CLASS] - odd[:, CLASS:]
                imag = even[:, CLASS:] + odd[:, :CLASS]
        square = real * real + imag * imag
        power = square if power is None else power + square
        spec.append((real, imag))
    group = BAND // FOLD
    same = (
        lax.broadcasted_iota(jnp.int32, (CLASS, CLASS), 0) // group
        == lax.broadcasted_iota(jnp.int32, (CLASS, CLASS), 1) // group
    )
    ones = jnp.where(same, 1.0, 0.0).astype(BF16)
    high = power.astype(BF16)
    low = (power - high.astype(F32)).astype(BF16)
    total = jnp.dot(high, ones, preferred_element_type=F32) + jnp.dot(
        low, ones, preferred_element_type=F32
    )
    factor = lax.rsqrt(total * (0.5 / BAND) + 1e-06)
    for r, (real, imag) in enumerate(spec):
        out_ref[:, r * PAIR : r * PAIR + CLASS] = (real * factor).astype(BF16)
        out_ref[:, r * PAIR + CLASS : (r + 1) * PAIR] = (imag * factor).astype(BF16)


def first_kernel(x_hbm, t_hbm, vis_hbm, out_ref, t_ref, vis_ref, x_ref, sem):
    copies = [
        pltpu.make_async_copy(x_hbm.at[0, 0], x_ref, sem.at[0]),
        pltpu.make_async_copy(t_hbm, t_ref, sem.at[1]),
        pltpu.make_async_copy(vis_hbm, vis_ref, sem.at[2]),
    ]
    for copy in copies:
        copy.start()
    for copy in copies:
        copy.wait()
    whiten(x_ref[...], t_ref, out_ref)


def second_kernel(first, count, x_hbm, t_ref, out_ref, rest_ref, x_ref, sem):
    segs, chans = x_hbm.shape[1], x_hbm.shape[2]
    copies = []
    for n in range(x_hbm.shape[0] * segs - first):
        target = x_ref.at[n] if n < count else rest_ref.at[n - count]
        unit = first + n
        copies.append(pltpu.make_async_copy(x_hbm.at[unit // segs, unit % segs], target, sem.at[n]))
    for copy in copies:
        copy.start()
    for copy in copies[:count]:
        copy.wait()
    whiten(x_ref[...].reshape(count * chans, NS), t_ref, out_ref)
    for copy in copies[count:]:
        copy.wait()


def later_kernel(x_ref, t_ref, out_ref):
    whiten(x_ref[...].reshape(out_ref.shape[0], NS), t_ref, out_ref)


def spectra_chunks(records, table, visits):
    days, segs, chans, _ = records.shape
    units = days * segs
    flops = 2 * chans * NS * WIDTH
    first, table, visits = call(
        first_kernel,
        [records, table, visits],
        (shape((chans, WIDTH)), shape(table.shape), shape(visits.shape, visits.dtype)),
        flops,
        [pltpu.VMEM((chans, NS), BF16), pltpu.SemaphoreType.DMA((3,))],
        hbm=3,
    )
    chunks = [first]
    count = max(units - 2, 1)
    left = units - 1 - count
    if units > 1:
        chunk, rest = call(
            functools.partial(second_kernel, 1, count),
            [records, table],
            (shape((count * chans, WIDTH)), shape((max(left, 1), chans, NS))),
            count * flops,
            [pltpu.VMEM((count, chans, NS), BF16), pltpu.SemaphoreType.DMA((units - 1,))],
            hbm=1,
        )
        chunks.append(chunk)
    if left:
        chunks.append(call(later_kernel, [rest, table], shape((left * chans, WIDTH)), left * flops))
    return chunks, visits


def one_hot(block, chans):
    row = jnp.concatenate([block[p : p + 1, :] for p in range(block.shape[0])], 1).astype(F32)
    chosen = lax.broadcasted_iota(jnp.int32, (chans, row.shape[1]), 0).astype(F32) == row
    return jnp.where(chosen, 1.0, 0.0).astype(F32).T.astype(BF16)


def cross_block(receivers, sources, select, r):
    cols = slice(r * PAIR, (r + 1) * PAIR)
    picks = select.shape[0] // receivers[0].shape[0]
    real = imag = None
    for own, other in zip(receivers, sources):
        g = jnp.dot(select, other[:, cols], preferred_element_type=F32)
        u = own[:, cols].astype(F32)
        u = jnp.concatenate([u] * picks, 0)
        ur, ui, gr, gi = u[:, :CLASS], u[:, CLASS:], g[:, :CLASS], g[:, CLASS:]
        a = ur * gr + ui * gi
        b = ur * gi - ui * gr
        real = a if real is None else real + a
        imag = b if imag is None else imag + b
    return jnp.concatenate([real, imag], 1).astype(BF16)


def lag_terms(inv_ref, jobs):
    total = None
    for r in range(FOLD):
        block = jnp.concatenate([cross_block(*job, r) for job in jobs], 0)
        part = lax.dot_general(
            inv_ref[:, r * PAIR : (r + 1) * PAIR],
            block,
            (((1,), (1,)), ((), ())),
            preferred_element_type=F32,
        )
        total = part if total is None else total + part
    return total


def units_of(ref, chans):
    return [ref.at[n * chans : (n + 1) * chans, :] for n in range(ref.shape[0] // chans)]


def center_kernel(inv_ref, vis_ref, *refs):
    chunks, out_ref, select_ref = refs[:-2], refs[-2], refs[-1]
    chans = vis_ref.shape[2]
    reach = vis_ref.shape[0] // 2
    units = [u for ref in chunks for u in units_of(ref, chans)]
    for n in range(reach):
        select_ref[n] = one_hot(vis_ref[reach - 1 - n], chans)
    out_ref[...] = lag_terms(inv_ref, [(units, units, one_hot(vis_ref[reach], chans))])


def select_kernel(wanted, *refs):
    out_ref = refs[-1]
    for n, (which, visit) in enumerate(wanted):
        out_ref[n] = one_hot(refs[which][visit], refs[which].shape[2])


def pair_kernel(jobs, n_blocks, inv_ref, near_ref, far_ref, *refs):
    blocks, out_ref = refs[:n_blocks], refs[-1]
    chans = near_ref.shape[2]
    units = [units_of(ref, chans) for ref in blocks]
    selects = (near_ref, far_ref)
    value = lag_terms(
        inv_ref,
        [(units[to], units[source], selects[k][n]) for to, source, k, n in jobs],
    )
    if len(refs) > n_blocks + 1:
        value = value + refs[n_blocks][...]
    out_ref[...] = value


def split_kernel(share, n_day, n_seg, n_parts, *refs):
    parts, keep_ref, send_ref = refs[:n_parts], refs[-2], refs[-1]
    day, seg = lax.axis_index("day"), lax.axis_index("seg")
    for ds in range(n_seg):
        for dd in range(n_day):
            block = lax.rem(day + dd, n_day) * n_seg + lax.rem(seg + ds, n_seg)
            rows = pl.ds(pl.multiple_of(block * share, share), share)
            at = 0
            for ref in parts:
                value = ref[rows, :]
                cols = slice(at, at + ref.shape[1])
                if ds == 0:
                    keep_ref[dd * share : (dd + 1) * share, cols] = value
                else:
                    send_ref[ds - 1, dd * share : (dd + 1) * share, cols] = value.astype(BF16)
                at += ref.shape[1]


def last_pair_kernel(pair_args, split_args, n_in, *refs):
    ins, parts, (keep_ref, send_ref, total) = refs[:n_in], refs[n_in:-3], refs[-3:]
    pair_kernel(*pair_args, *ins, total)
    split_kernel(*split_args, *parts, total, keep_ref, send_ref)


def merge_kernel(share, wide, groups, n_got, *refs):
    keep_ref, got, outs = refs[0], refs[1 : 1 + n_got], refs[1 + n_got :]
    n_day = keep_ref.shape[0] // share
    for dd in range(n_day):
        rows = slice(dd * share, (dd + 1) * share)
        for g, group in enumerate(groups):
            for place, n in enumerate(group):
                cols = slice(n * wide, (n + 1) * wide)
                value = keep_ref[rows, cols]
                for ref in got:
                    value = value + ref[rows, cols].astype(F32)
                to = slice(place * wide, (place + 1) * wide)
                if g == 0 and dd == 0:
                    outs[0][:, to] = value
                elif g == 0:
                    outs[1][dd - 1, :, to] = value.astype(BF16)
                else:
                    outs[g + 1][dd, :, to] = value.astype(BF16)


def ring_plan(n_chan, reach):
    groups, routes = [], []
    for o in range(1, reach + 1):
        to = [((i + o) % n_chan, i) for i in range(n_chan)]
        routes.append([(j, i) for i, j in to])
        jobs = [(0, 1, 0, o - 1), (1, 0, 1, 0)]
        groups.append(([to], [(0, reach + o)], jobs, [reach - o, reach + o], [None, o - 1]))
    return groups, routes


def local(records, visits):
    day_local, _, chans, _ = records.shape
    visit_count, picks, _ = visits.shape
    reach = visit_count // 2
    n_chan, n_day, n_seg = (lax.axis_size(a) for a in ("chan", "day", "seg"))
    share = LAGS // (n_day * n_seg)
    wide = picks * chans
    table = trig_columns(np.arange(SPAN)).reshape(SPAN, FOLD, PAIR).transpose(1, 0, 2)
    table = jnp.asarray(np.ascontiguousarray(table))
    inverse = jnp.asarray(trig_columns(np.arange(LAGS) - LAGS // 2))
    plan, routes = ring_plan(n_chan, reach)

    chunks, visits = spectra_chunks(records, table, visits)
    held, asked = [], []
    for arrivals, *_ in plan:
        held.append([[lax.ppermute(c, "chan", to) for to in arrivals] for c in chunks])
        asked.append([lax.ppermute(visits, "chan", to) for to in arrivals])

    flops = 2 * wide * LAGS * WIDTH
    center, near = call(
        center_kernel,
        [inverse, visits, *chunks],
        (shape((LAGS, wide), F32), shape((reach, wide, chans))),
        flops,
    )
    parts = [center]
    visit_of, way_of = [reach], [None]
    for g, (arrivals, wanted, jobs, visits_of, ways) in enumerate(plan):
        visit_of += visits_of
        way_of += ways
        far = call(
            functools.partial(select_kernel, wanted), asked[g], shape((len(wanted), wide, chans)), 0
        )
        total = None
        for n, chunk in enumerate(chunks):
            args = (jobs, 1 + len(arrivals))
            ops = [inverse, near, far, chunk, *held[g][n]] + ([] if total is None else [total])
            if g == len(plan) - 1 and n == len(chunks) - 1:
                cols = len(visit_of) * wide
                keep, send = call(
                    functools.partial(
                        last_pair_kernel, args, (share, n_day, n_seg, len(parts) + 1), len(ops)
                    ),
                    ops + parts,
                    (
                        shape((n_day * share, cols), F32),
                        shape((n_seg - 1, n_day * share, cols)),
                    ),
                    len(jobs) * flops,
                    [pltpu.VMEM((LAGS, len(jobs) * wide), F32)],
                )
            else:
                total = call(
                    functools.partial(pair_kernel, *args),
                    ops,
                    shape((LAGS, len(jobs) * wide), F32),
                    len(jobs) * flops,
                )
        parts.append(total)

    got = []
    for ds in range(1, n_seg):
        route = [(i, (i + ds) % n_seg) for i in range(n_seg)]
        got.append(lax.ppermute(send[ds - 1], "seg", route))
    groups = [[n for n, way in enumerate(way_of) if way is None]]
    groups += [[n for n, way in enumerate(way_of) if way == k] for k in range(len(routes))]
    own, by_day, *away = call(
        functools.partial(merge_kernel, share, wide, groups, len(got)),
        [keep, *got],
        (
            shape((share, len(groups[0]) * wide), F32),
            shape((max(n_day - 1, 1), share, len(groups[0]) * wide)),
            *[shape((n_day, share, len(g) * wide)) for g in groups[1:]],
        ),
        0,
    )
    columns = [None] * visit_count

    def add(group, values):
        for place, n in enumerate(group):
            v = visit_of[n]
            value = values[:, place * wide : (place + 1) * wide].astype(F32)
            columns[v] = value if columns[v] is None else columns[v] + value

    for k, pairs in enumerate(routes):
        for dd in range(n_day):
            route = [
                (i * n_day + d, j * n_day + (d + dd) % n_day) for i, j in pairs for d in range(n_day)
            ]
            add(groups[k + 1], lax.ppermute(away[k][dd], ("chan", "day"), route))
    for dd in range(1, n_day):
        route = [(i, (i + dd) % n_day) for i in range(n_day)]
        add(groups[0], lax.ppermute(by_day[dd - 1], "day", route))
    add(groups[0], own)
    days_all = day_local * n_day
    scale = 1.0 / math.sqrt(FREQS * days_all * SEGS)
    result = (jnp.concatenate(columns, 1) * scale).astype(BF16)
    return result.reshape(share, visit_count, picks, chans)


def solution(mesh):
    in_specs = (P("day", "seg", ("grp", "chan"), None), P(None, None, ("grp", "chan")))
    out_specs = P(("day", "seg"), None, None, ("grp", "chan"))

    return jax.shard_map(local, mesh=mesh, in_specs=in_specs, out_specs=out_specs, check_vma=False)
```

```python
import functools
import math

import jax
import jax.numpy as jnp
import numpy as np
from jax import lax
from jax.experimental import pallas as pl
from jax.experimental.pallas import tpu as pltpu
from jax.sharding import PartitionSpec as P


NS = 2048
FREQS = 512
BAND = 64
LAGS = 256
SEGS = 4
FOLD = 4
SPAN = NS // FOLD
CLASS = FREQS // FOLD
PAIR = 2 * CLASS
WIDTH = 2 * FREQS
GRANT = 24 << 20
BF16 = jnp.bfloat16
F32 = jnp.float32


def trig_columns(index):
    blocks = []
    for r in range(FOLD):
        freqs = FOLD * np.arange(CLASS) + r
        turns = (index[:, None] * freqs[None, :] % NS) * (2.0 * math.pi / NS)
        blocks += [np.cos(turns), -np.sin(turns)]
    return np.concatenate(blocks, 1).astype(jnp.bfloat16)


def in_vmem():
    return pl.BlockSpec(memory_space=pltpu.VMEM)


def cost(flops, ops):
    size = sum(int(np.prod(op.shape)) * op.dtype.itemsize for op in ops)
    return pl.CostEstimate(flops=flops, bytes_accessed=size, transcendentals=0)


def call(kernel, ops, out_shape, flops, scratch=(), hbm=0):
    ops = [pltpu.with_memory_space_constraint(op, pltpu.HBM) for op in ops[:hbm]] + ops[hbm:]
    return pl.pallas_call(
        kernel,
        out_shape=out_shape,
        in_specs=[pl.BlockSpec(memory_space=pltpu.HBM)] * hbm + [in_vmem() for _ in ops[hbm:]],
        out_specs=jax.tree.map(lambda s: in_vmem(), out_shape),
        scratch_shapes=list(scratch),
        cost_estimate=cost(flops, ops),
        compiler_params=pltpu.CompilerParams(vmem_limit_bytes=GRANT),
    )(*ops)


def shape(dims, dtype=BF16):
    return jax.ShapeDtypeStruct(dims, dtype)


def whiten(x, t_ref, out_ref):
    rows = x.shape[0]
    stacked = jnp.concatenate([x[:, q * SPAN : (q + 1) * SPAN] for q in range(FOLD)], 0)
    spec = []
    power = None
    for r in range(FOLD):
        product = jnp.dot(stacked, t_ref[r], preferred_element_type=F32)
        p = [product[q * rows : (q + 1) * rows] for q in range(FOLD)]
        if r % 2 == 0:
            even, odd = p[0] + p[2], p[1] + p[3]
            both = even + odd if r == 0 else even - odd
            real, imag = both[:, :CLASS], both[:, CLASS:]
        else:
            even, odd = p[0] - p[2], p[1] - p[3]
            if r == 1:
                real = even[:, :CLASS] + odd[:, CLASS:]
                imag = even[:, CLASS:] - odd[:, :CLASS]
            else:
                real = even[:, :CLASS] - odd[:, CLASS:]
                imag = even[:, CLASS:] + odd[:, :CLASS]
        square = real * real + imag * imag
        power = square if power is None else power + square
        spec.append((real, imag))
    group = BAND // FOLD
    same = (
        lax.broadcasted_iota(jnp.int32, (CLASS, CLASS), 0) // group
        == lax.broadcasted_iota(jnp.int32, (CLASS, CLASS), 1) // group
    )
    ones = jnp.where(same, 1.0, 0.0).astype(BF16)
    high = power.astype(BF16)
    low = (power - high.astype(F32)).astype(BF16)
    total = jnp.dot(high, ones, preferred_element_type=F32) + jnp.dot(
        low, ones, preferred_element_type=F32
    )
    factor = lax.rsqrt(total * (0.5 / BAND) + 1e-06)
    for r, (real, imag) in enumerate(spec):
        out_ref[:, r * PAIR : r * PAIR + CLASS] = (real * factor).astype(BF16)
        out_ref[:, r * PAIR + CLASS : (r + 1) * PAIR] = (imag * factor).astype(BF16)


def first_kernel(x_hbm, t_hbm, vis_hbm, out_ref, t_ref, vis_ref, x_ref, sem):
    copies = [
        pltpu.make_async_copy(x_hbm.at[0, 0], x_ref, sem.at[0]),
        pltpu.make_async_copy(t_hbm, t_ref, sem.at[1]),
        pltpu.make_async_copy(vis_hbm, vis_ref, sem.at[2]),
    ]
    for copy in copies:
        copy.start()
    for copy in copies:
        copy.wait()
    whiten(x_ref[...], t_ref, out_ref)


def second_kernel(first, count, x_hbm, t_ref, out_ref, rest_ref, x_ref, sem):
    segs, chans = x_hbm.shape[1], x_hbm.shape[2]
    copies = []
    for n in range(x_hbm.shape[0] * segs - first):
        target = x_ref.at[n] if n < count else rest_ref.at[n - count]
        unit = first + n
        copies.append(pltpu.make_async_copy(x_hbm.at[unit // segs, unit % segs], target, sem.at[n]))
    for copy in copies:
        copy.start()
    for copy in copies[:count]:
        copy.wait()
    whiten(x_ref[...].reshape(count * chans, NS), t_ref, out_ref)
    for copy in copies[count:]:
        copy.wait()


def later_kernel(x_ref, t_ref, out_ref):
    whiten(x_ref[...].reshape(out_ref.shape[0], NS), t_ref, out_ref)


def spectra_chunks(records, table, visits):
    days, segs, chans, _ = records.shape
    units = days * segs
    flops = 2 * chans * NS * WIDTH
    first, table, visits = call(
        first_kernel,
        [records, table, visits],
        (shape((chans, WIDTH)), shape(table.shape), shape(visits.shape, visits.dtype)),
        flops,
        [pltpu.VMEM((chans, NS), BF16), pltpu.SemaphoreType.DMA((3,))],
        hbm=3,
    )
    chunks = [first]
    count = max(units - 2, 1)
    left = units - 1 - count
    if units > 1:
        chunk, rest = call(
            functools.partial(second_kernel, 1, count),
            [records, table],
            (shape((count * chans, WIDTH)), shape((max(left, 1), chans, NS))),
            count * flops,
            [pltpu.VMEM((count, chans, NS), BF16), pltpu.SemaphoreType.DMA((units - 1,))],
            hbm=1,
        )
        chunks.append(chunk)
    if left:
        chunks.append(call(later_kernel, [rest, table], shape((left * chans, WIDTH)), left * flops))
    return chunks, visits


def one_hot(block, chans):
    row = jnp.concatenate([block[p : p + 1, :] for p in range(block.shape[0])], 1).astype(F32)
    chosen = lax.broadcasted_iota(jnp.int32, (chans, row.shape[1]), 0).astype(F32) == row
    return jnp.where(chosen, 1.0, 0.0).astype(F32).T.astype(BF16)


def cross_block(receivers, sources, select, r):
    cols = slice(r * PAIR, (r + 1) * PAIR)
    picks = select.shape[0] // receivers[0].shape[0]
    real = imag = None
    for own, other in zip(receivers, sources):
        g = jnp.dot(select, other[:, cols], preferred_element_type=F32)
        u = own[:, cols].astype(F32)
        u = jnp.concatenate([u] * picks, 0)
        ur, ui, gr, gi = u[:, :CLASS], u[:, CLASS:], g[:, :CLASS], g[:, CLASS:]
        a = ur * gr + ui * gi
        b = ur * gi - ui * gr
        real = a if real is None else real + a
        imag = b if imag is None else imag + b
    return jnp.concatenate([real, imag], 1).astype(BF16)


def lag_terms(inv_ref, jobs):
    total = None
    for r in range(FOLD):
        block = jnp.concatenate([cross_block(*job, r) for job in jobs], 0)
        part = lax.dot_general(
            inv_ref[:, r * PAIR : (r + 1) * PAIR],
            block,
            (((1,), (1,)), ((), ())),
            preferred_element_type=F32,
        )
        total = part if total is None else total + part
    return total


def units_of(ref, chans):
    return [ref.at[n * chans : (n + 1) * chans, :] for n in range(ref.shape[0] // chans)]


def center_kernel(inv_ref, vis_ref, *refs):
    chunks, out_ref, select_ref = refs[:-2], refs[-2], refs[-1]
    chans = vis_ref.shape[2]
    reach = vis_ref.shape[0] // 2
    units = [u for ref in chunks for u in units_of(ref, chans)]
    for n in range(reach):
        select_ref[n] = one_hot(vis_ref[reach + 1 + n], chans)
    out_ref[...] = lag_terms(inv_ref, [(units, units, one_hot(vis_ref[reach], chans))])


def select_kernel(wanted, *refs):
    out_ref = refs[-1]
    for n, (which, visit) in enumerate(wanted):
        out_ref[n] = one_hot(refs[which][visit], refs[which].shape[2])


def pair_kernel(jobs, n_blocks, inv_ref, near_ref, far_ref, *refs):
    blocks, out_ref = refs[:n_blocks], refs[-1]
    chans = near_ref.shape[2]
    units = [units_of(ref, chans) for ref in blocks]
    selects = (near_ref, far_ref)
    value = lag_terms(
        inv_ref,
        [(units[to], units[source], selects[k][n]) for to, source, k, n in jobs],
    )
    if len(refs) > n_blocks + 1:
        value = value + refs[n_blocks][...]
    out_ref[...] = value


def split_kernel(share, n_day, n_seg, n_parts, *refs):
    parts, keep_ref, send_ref = refs[:n_parts], refs[-2], refs[-1]
    day, seg = lax.axis_index("day"), lax.axis_index("seg")
    for ds in range(n_seg):
        for dd in range(n_day):
            block = lax.rem(day + dd, n_day) * n_seg + lax.rem(seg + ds, n_seg)
            rows = pl.ds(pl.multiple_of(block * share, share), share)
            at = 0
            for ref in parts:
                value = ref[rows, :]
                cols = slice(at, at + ref.shape[1])
                if ds == 0:
                    keep_ref[dd * share : (dd + 1) * share, cols] = value
                else:
                    send_ref[ds - 1, dd * share : (dd + 1) * share, cols] = value.astype(BF16)
                at += ref.shape[1]


def last_pair_kernel(pair_args, split_args, n_in, *refs):
    ins, parts, (keep_ref, send_ref, total) = refs[:n_in], refs[n_in:-3], refs[-3:]
    pair_kernel(*pair_args, *ins, total)
    split_kernel(*split_args, *parts, total, keep_ref, send_ref)


def merge_kernel(share, wide, groups, n_got, *refs):
    keep_ref, got, outs = refs[0], refs[1 : 1 + n_got], refs[1 + n_got :]
    n_day = keep_ref.shape[0] // share
    for dd in range(n_day):
        rows = slice(dd * share, (dd + 1) * share)
        for g, group in enumerate(groups):
            for place, n in enumerate(group):
                cols = slice(n * wide, (n + 1) * wide)
                value = keep_ref[rows, cols]
                for ref in got:
                    value = value + ref[rows, cols].astype(F32)
                to = slice(place * wide, (place + 1) * wide)
                if g == 0 and dd == 0:
                    outs[0][:, to] = value
                elif g == 0:
                    outs[1][dd - 1, :, to] = value.astype(BF16)
                else:
                    outs[g + 1][dd, :, to] = value.astype(BF16)


def ring_plan(n_chan, reach):
    groups, routes = [], []
    for o in range(1, reach + 1):
        to = [(i, (i + o) % n_chan) for i in range(n_chan)]
        routes.append([(j, i) for i, j in to])
        jobs = [(0, 1, 0, o - 1), (1, 0, 1, 0)]
        groups.append(([to], [(0, reach - o)], jobs, [reach + o, reach - o], [None, o - 1]))
    return groups, routes


def local(records, visits):
    day_local, _, chans, _ = records.shape
    visit_count, picks, _ = visits.shape
    reach = visit_count // 2
    n_chan, n_day, n_seg = (lax.axis_size(a) for a in ("chan", "day", "seg"))
    share = LAGS // (n_day * n_seg)
    wide = picks * chans
    table = trig_columns(np.arange(SPAN)).reshape(SPAN, FOLD, PAIR).transpose(1, 0, 2)
    table = jnp.asarray(np.ascontiguousarray(table))
    inverse = jnp.asarray(trig_columns(np.arange(LAGS) - LAGS // 2))
    plan, routes = ring_plan(n_chan, reach)

    chunks, visits = spectra_chunks(records, table, visits)
    held, asked = [], []
    for arrivals, *_ in plan:
        held.append([[lax.ppermute(c, "chan", to) for to in arrivals] for c in chunks])
        asked.append([lax.ppermute(visits, "chan", to) for to in arrivals])

    flops = 2 * wide * LAGS * WIDTH
    center, near = call(
        center_kernel,
        [inverse, visits, *chunks],
        (shape((LAGS, wide), F32), shape((reach, wide, chans))),
        flops,
    )
    parts = [center]
    visit_of, way_of = [reach], [None]
    for g, (arrivals, wanted, jobs, visits_of, ways) in enumerate(plan):
        visit_of += visits_of
        way_of += ways
        far = call(
            functools.partial(select_kernel, wanted), asked[g], shape((len(wanted), wide, chans)), 0
        )
        total = None
        for n, chunk in enumerate(chunks):
            args = (jobs, 1 + len(arrivals))
            ops = [inverse, near, far, chunk, *held[g][n]] + ([] if total is None else [total])
            if g == len(plan) - 1 and n == len(chunks) - 1:
                cols = len(visit_of) * wide
                keep, send = call(
                    functools.partial(
                        last_pair_kernel, args, (share, n_day, n_seg, len(parts) + 1), len(ops)
                    ),
                    ops + parts,
                    (
                        shape((n_day * share, cols), F32),
                        shape((n_seg - 1, n_day * share, cols)),
                    ),
                    len(jobs) * flops,
                    [pltpu.VMEM((LAGS, len(jobs) * wide), F32)],
                )
            else:
                total = call(
                    functools.partial(pair_kernel, *args),
                    ops,
                    shape((LAGS, len(jobs) * wide), F32),
                    len(jobs) * flops,
                )
        parts.append(total)

    got = []
    for ds in range(1, n_seg):
        route = [(i, (i + ds) % n_seg) for i in range(n_seg)]
        got.append(lax.ppermute(send[ds - 1], "seg", route))
    groups = [[n for n, way in enumerate(way_of) if way is None]]
    groups += [[n for n, way in enumerate(way_of) if way == k] for k in range(len(routes))]
    own, by_day, *away = call(
        functools.partial(merge_kernel, share, wide, groups, len(got)),
        [keep, *got],
        (
            shape((share, len(groups[0]) * wide), F32),
            shape((max(n_day - 1, 1), share, len(groups[0]) * wide)),
            *[shape((n_day, share, len(g) * wide)) for g in groups[1:]],
        ),
        0,
    )
    columns = [None] * visit_count

    def add(group, values):
        for place, n in enumerate(group):
            v = visit_of[n]
            value = values[:, place * wide : (place + 1) * wide].astype(F32)
            columns[v] = value if columns[v] is None else columns[v] + value

    for k, pairs in enumerate(routes):
        for dd in range(n_day):
            route = [
                (i * n_day + d, j * n_day + (d + dd) % n_day) for i, j in pairs for d in range(n_day)
            ]
            add(groups[k + 1], lax.ppermute(away[k][dd], ("chan", "day"), route))
    for dd in range(1, n_day):
        route = [(i, (i + dd) % n_day) for i in range(n_day)]
        add(groups[0], lax.ppermute(by_day[dd - 1], "day", route))
    add(groups[0], own)
    days_all = day_local * n_day
    scale = 1.0 / math.sqrt(FREQS * days_all * SEGS)
    result = (jnp.concatenate(columns, 1) * scale).astype(BF16)
    return result.reshape(share, visit_count, picks, chans)


def solution(mesh):
    in_specs = (P("day", "seg", ("grp", "chan"), None), P(None, None, ("grp", "chan")))
    out_specs = P(("day", "seg"), None, None, ("grp", "chan"))

    return jax.shard_map(local, mesh=mesh, in_specs=in_specs, out_specs=out_specs, check_vma=False)
```
